32 devices in a mesh: rep: 8 (over y, x, core), shard: 4 (over z).
Axes of the slice: x: 2, y: 2, z: 4, core: 2. Of those that a mesh axis runs over, the one named last changes fastest.
Arguments:
- tokens: bfloat16 [8, 1024, 2048], P('rep', 'shard'), may hold values from -6 to 6
- segments: int32 [8, 1024], P('rep'), may hold values from 0 to 15, as said below
- positions: int32 [8, 1024], P('rep', 'shard'), may hold values from 0 to 1023, as said below
- norm_gain: bfloat16 [2048], P('shard'), may hold values from 0.5 to 1.5
- norm_shift: bfloat16 [2048], P('shard'), may hold values from -1.75 to 1.75
- inproj_weight: bfloat16 [6144, 2048], P('shard'), may hold values from -0.125 to 0.125
- inproj_bias: bfloat16 [6144], P('shard'), may hold values from -3 to 3
- outproj_weight: bfloat16 [2048, 2048], P('shard'), may hold values from -0.75 to 0.75
- outproj_bias: bfloat16 [2048], P('shard'), may hold values from -3 to 3
- expand_weight: bfloat16 [8192, 2048], P('shard'), may hold values from -0.125 to 0.125
- expand_bias: bfloat16 [8192], P('shard'), may hold values from -3 to 3
- shrink_weight: bfloat16 [2048, 8192], P('shard'), may hold values from -0.0625 to 0.0625
- shrink_bias: bfloat16 [2048], P('shard'), may hold values from -3 to 3
- out_grad: bfloat16 [8, 1024, 2048], P('rep', 'shard'), may hold values from -6 to 6
Outputs:
- block_output: bfloat16 [8, 1024, 2048], P('rep', 'shard')
- token_grad: float32 [8, 1024, 2048], P('rep', 'shard')
- grad_gain: float32 [2048], P('shard')
- grad_shift: float32 [2048], P('shard')
- grad_inproj: float32 [6144, 2048], P('shard')
- grad_inbias: float32 [6144], P('shard')
- grad_outproj: float32 [2048, 2048], P('shard')
- grad_outbias: float32 [2048], P('shard')
- grad_expand: float32 [8192, 2048], P('shard')
- grad_expbias: float32 [8192], P('shard')
- grad_shrink: float32 [2048, 8192], P('shard')
- grad_shrbias: float32 [2048], P('shard')
The draws below stay inside these ranges and needn't reach their ends.
Inputs may be any that keep to these rules, and one draw needn't show every extreme that they name: `segments`: along each row the document numbers start at 0 and never fall; a document starts only at a multiple of 64 positions. `positions`: each token's offset from the first token of its document.
All inputs are finite; a program needn't handle non-finite values.
Results may differ from the reference program's by a relative error of at most 0.011.
Values may be sent and summed in bfloat16 or wider, within the bound.
No kernel may reach another device: no remote copies, remote signals or barrier semaphores. Data moves between devices by JAX's collectives and lax.ppermute only.
A program may use at most 640 MiB of HBM per device.

```python
import math
import jax
import jax.numpy as jnp
from jax import lax

D = 2048
HEADS = 32
HEAD_DIM = 64
ROT = 32
FF = 8192
LEN = 1024
ROWS = 8


def documents(key):
    places = jnp.arange(LEN, dtype=jnp.int32)
    spacing = LEN // 16
    row_ids = jnp.arange(ROWS, dtype=jnp.int32)
    coins = jax.random.randint(jax.random.fold_in(key, 5), (ROWS, 16), 0, 3) == 0
    coins = jnp.logical_or(coins, row_ids[:, None] == ROWS - 1)
    coins = jnp.logical_and(coins, row_ids[:, None] != 0)
    spread_coins = jnp.repeat(coins, spacing, axis=1)
    on_grid = places % spacing == 0
    boundary = jnp.logical_and(spread_coins, on_grid[None, :])
    boundary = jnp.logical_or(boundary, places[None, :] == 0)
    segment_ids = jnp.cumsum(boundary.astype(jnp.int32), axis=1) - 1
    starts = lax.cummax(jnp.where(boundary, places[None, :], 0), axis=1)
    return (segment_ids.astype(jnp.int32), (places[None, :] - starts).astype(jnp.int32))


def draw_segments(key, part):
    return documents(key)[0]


def draw_positions(key, part):
    return documents(key)[1]


def steps_of(key, shape, split, smallest, top_value):
    level, own = 1.0, jax.random.fold_in(key, 6)
    for position, shards_of in split:
        heights = jnp.exp(jax.random.uniform(jax.random.fold_in(own, position), (shards_of,), jnp.float32, smallest / len(split), top_value / len(split)))
        level = level * jnp.repeat(heights, shape[position] // shards_of).reshape([-1 if axis == position else 1 for axis in range(len(shape))])
    return level


def centred(own_key, dims, deviation, reach, pieces=(), kind=jnp.bfloat16):
    loudness = steps_of(own_key, dims, pieces, -0.22, 0.18) if pieces else 1.0
    array = jax.random.normal(own_key, dims, jnp.float32) * deviation * loudness
    return jnp.minimum(jnp.maximum(array, -reach), reach).astype(kind)


def setup_inputs(seed: int = 0) -> dict:
    arg_keys = jax.random.split(jax.random.key(seed), 15)
    return {
        "tokens": centred(arg_keys[0], (ROWS, LEN, D), 1.0, 6.0, ((0, 8), (1, 4))),
        "segments": draw_segments(jax.random.fold_in(arg_keys[14], 71), 0),
        "positions": draw_positions(jax.random.fold_in(arg_keys[14], 71), 0),
        "norm_gain": jnp.clip(1.0 + 0.1 * jax.random.normal(arg_keys[3], (D,), jnp.float32), 0.5, 1.5).astype(jnp.bfloat16),
        "norm_shift": centred(arg_keys[4], (D,), 0.3, 1.75, ((0, 4),)),
        "inproj_weight": centred(arg_keys[5], (3 * D, D), D ** -0.5, 0.125, ((0, 4),)),
        "inproj_bias": centred(arg_keys[6], (3 * D,), 0.5, 3.0, ((0, 4),)),
        "outproj_weight": centred(arg_keys[7], (D, D), (D // 32) ** -0.5, 0.75, ((0, 4),)),
        "outproj_bias": centred(arg_keys[8], (D,), 0.5, 3.0, ((0, 4),)),
        "expand_weight": centred(arg_keys[9], (FF, D), D ** -0.5, 0.125, ((0, 4),)),
        "expand_bias": centred(arg_keys[10], (FF,), 0.5, 3.0, ((0, 4),)),
        "shrink_weight": centred(arg_keys[11], (D, FF), FF ** -0.5, 0.0625, ((0, 4),)),
        "shrink_bias": centred(arg_keys[12], (D,), 0.5, 3.0, ((0, 4),)),
        "out_grad": centred(arg_keys[13], (ROWS, LEN, D), 1.0, 6.0, ((0, 8), (1, 4))),
    }


@jax.custom_vjp
def low(v):
    return lax.optimization_barrier(v.astype(jnp.bfloat16)).astype(jnp.float32)

@jax.custom_vjp
def low_back(v):
    return v

def low_keep(v):
    return (low(v), None)

def low_pass(kept, grad):
    return (grad,)

def back_keep(v):
    return (v, None)

def back_low(kept, grad):
    return (low(grad),)
low.defvjp(low_keep, low_pass)
low_back.defvjp(back_keep, back_low)

def project(values, weight):
    return jnp.dot(values, weight.T, precision=lax.Precision.HIGHEST)

def gelu_tanh(values):
    return 0.5 * values * (1.0 + jnp.tanh(math.sqrt(2.0 / math.pi) * (values + 0.044715 * values * values * values)))

def rotate(values, cosine, sine):
    rot_half = ROT // 2
    first_part = values[..., :rot_half]
    second_part = values[..., rot_half:ROT]
    return jnp.concatenate([first_part * cosine - second_part * sine, second_part * cosine + first_part * sine, values[..., ROT:]], -1)

def row_forward(params, row_tokens, row_segments, row_positions):
    gain, shift, in_weight, in_bias, out_weight, out_bias, up_weight, up_bias, down_weight, down_bias = params
    row_mean = lax.optimization_barrier(jnp.mean(row_tokens, -1, keepdims=True))
    centered_rows = row_tokens - row_mean
    row_var = lax.optimization_barrier(jnp.mean(centered_rows * centered_rows, -1, keepdims=True))
    normalized_rows = low(centered_rows * lax.rsqrt(row_var + 1e-05) * gain + shift)
    mixed = low_back(project(normalized_rows, in_weight) + in_bias)
    queries = mixed[:, :D].reshape(LEN, HEADS, HEAD_DIM)
    key_part = mixed[:, D:2 * D].reshape(LEN, HEADS, HEAD_DIM)
    values = mixed[:, 2 * D:].reshape(LEN, HEADS, HEAD_DIM)
    inverse_freq = 10000.0 ** (-jnp.arange(ROT // 2).astype(jnp.float32) * 2.0 / ROT)
    angle = row_positions.astype(jnp.float32)[:, None, None] * inverse_freq[None, None, :]
    cosine = jnp.cos(angle)
    sine = jnp.sin(angle)
    q_rot = low(rotate(queries, cosine, sine))
    k_rot = low(rotate(key_part, cosine, sine))
    v_low = low(values)
    scores = jnp.einsum('qhd,khd->hqk', q_rot, k_rot, precision=lax.Precision.HIGHEST) * HEAD_DIM ** (-0.5)
    places = jnp.arange(LEN)
    allowed = (places[None, :] <= places[:, None]) & (row_segments[None, :] == row_segments[:, None])
    scores = low_back(jnp.where(allowed[None], scores, -1e+30))
    probs = jax.nn.softmax(scores, axis=-1)
    attended = jnp.einsum('hqk,khd->qhd', low(probs), v_low, precision=lax.Precision.HIGHEST).reshape(LEN, D)
    attended = low(low_back(attended))
    hidden = low(gelu_tanh(low_back(project(normalized_rows, up_weight) + up_bias)))
    branches = low_back(project(attended, out_weight) + out_bias + project(hidden, down_weight) + down_bias)
    return row_tokens + branches

def reference(tokens, segments, positions, norm_gain, norm_shift, inproj_weight, inproj_bias, outproj_weight, outproj_bias, expand_weight, expand_bias, shrink_weight, shrink_bias, out_grad):
    params = (norm_gain.astype(jnp.float32), norm_shift.astype(jnp.float32), inproj_weight.astype(jnp.float32), inproj_bias.astype(jnp.float32), outproj_weight.astype(jnp.float32), outproj_bias.astype(jnp.float32), expand_weight.astype(jnp.float32), expand_bias.astype(jnp.float32), shrink_weight.astype(jnp.float32), shrink_bias.astype(jnp.float32))
    tokens_f = tokens.astype(jnp.float32)

    def forward(params, tokens_f):

        def one_row(packed):
            return jax.checkpoint(row_forward)(params, packed[0], packed[1], packed[2])
        return lax.map(one_row, (tokens_f, segments, positions))
    outputs, pullback = jax.vjp(forward, params, tokens_f)
    grads, token_grad = pullback(out_grad.astype(jnp.float32))
    return (outputs.astype(jnp.bfloat16), token_grad, grads[0], grads[1], grads[2], grads[3], grads[4], grads[5], grads[6], grads[7], grads[8], grads[9])
```

```python
import functools
import math

import jax
import jax.numpy as jnp
import numpy as np
from jax import lax
from jax.experimental import pallas as pl
from jax.experimental.pallas import tpu as pltpu
from jax.sharding import PartitionSpec as P


HEAD_DIM = 64
ROT = 32
PAIR = 2 * HEAD_DIM
NEG = -1e30
F32 = jnp.float32
BF16 = jnp.bfloat16


def nt(a, b):
    return lax.dot_general(a, b, (((1,), (1,)), ((), ())), preferred_element_type=F32)


def nn(a, b):
    return lax.dot_general(a, b, (((1,), (0,)), ((), ())), preferred_element_type=F32)


def tn(a, b):
    return lax.dot_general(a, b, (((0,), (0,)), ((), ())), preferred_element_type=F32)


def gelu_parts(values):
    c = math.sqrt(2.0 / math.pi)
    square = values * values
    t = jnp.tanh(c * (values + 0.044715 * square * values))
    half = 0.5 * (1.0 + t)
    slope = half + 0.5 * values * (1.0 - t * t) * (c * (1.0 + 3.0 * 0.044715 * square))
    return values * half, slope


def rotate_pair(x, cosine, sine_low, sine_high):
    quarter = ROT // 2
    up = pltpu.roll(x, PAIR - quarter, 1)
    down = pltpu.roll(x, quarter, 1)
    return x * cosine + up * sine_low + down * sine_high


def allowed_mask(seg_col, seg_row, first_key, keys, first_query, queries):
    same = seg_col == seg_row
    kpos = first_key + lax.broadcasted_iota(jnp.int32, (keys, queries), 0)
    qpos = first_query + lax.broadcasted_iota(jnp.int32, (keys, queries), 1)
    return same & (kpos <= qpos)


def attend_kernel(blk, q_ref, k_ref, v_ref, cos_ref, slo_ref, shi_ref, segc_ref, segr_ref,
                  o_ref, q_out, k_out, v_out, lse_ref):
    length = q_ref.shape[0]
    cosine, slo, shi = cos_ref[...], slo_ref[...], shi_ref[...]
    q_low = (rotate_pair(q_ref[...], cosine, slo, shi).astype(BF16)) * jnp.asarray(HEAD_DIM**-0.5, BF16)
    k_low = rotate_pair(k_ref[...], cosine, slo, shi).astype(BF16)
    v_low = v_ref[...].astype(BF16)
    q_out[...] = q_low
    k_out[...] = k_low
    v_out[...] = v_low
    lane = lax.broadcasted_iota(jnp.int32, (1, PAIR), 1)
    v_t = v_low.T
    for b in range(length // blk):
        rows = slice(b * blk, (b + 1) * blk)
        keys = (b + 1) * blk
        mask = allowed_mask(segc_ref[:keys, :1], segr_ref[:1, rows], 0, keys, b * blk, blk)
        outs = []
        for h in range(2):
            mine = (lane < HEAD_DIM) if h == 0 else (lane >= HEAD_DIM)
            qh = jnp.where(mine, q_low[rows], jnp.zeros((), BF16))
            s = jnp.where(mask, nt(k_low[:keys], qh), NEG)
            top = jnp.max(s, axis=0, keepdims=True)
            e = jnp.exp(s - top)
            total = jnp.sum(e, axis=0, keepdims=True)
            p = (e * (1.0 / total)).astype(BF16)
            lse_ref[0, h : h + 1, rows] = top + jnp.log(total)
            outs.append(nn(v_t[h * HEAD_DIM : (h + 1) * HEAD_DIM, :keys], p))
        o_ref[rows, :] = jnp.concatenate(outs, 0).T.astype(BF16)


def attend(mixed, tables, seg_col, seg_row, blk):
    length, wide = mixed.shape
    heads_wide = wide // 3
    pairs = heads_wide // PAIR
    col = lambda off: pl.BlockSpec((length, PAIR), lambda p: (0, off + p))
    fixed = lambda shape: pl.BlockSpec(shape, lambda p: (0, 0))
    return pl.pallas_call(
        functools.partial(attend_kernel, blk),
        grid=(pairs,),
        in_specs=[col(0), col(pairs), col(2 * pairs)]
        + [fixed((length, PAIR))] * 3
        + [fixed((length, 1)), fixed((1, length))],
        out_specs=[col(0)] * 4 + [pl.BlockSpec((1, 2, length), lambda p: (p, 0, 0))],
        out_shape=[jax.ShapeDtypeStruct((length, heads_wide), BF16)] * 4
        + [jax.ShapeDtypeStruct((pairs, 2, length), F32)],
        compiler_params=pltpu.CompilerParams(vmem_limit_bytes=56 << 20),
        name="attend",
    )(mixed, mixed, mixed, *tables, seg_col, seg_row)


def attend_back_kernel(blk, q_ref, k_ref, v_ref, g_ref, lse_ref, cos_ref, slo_ref, shi_ref,
                       segc_ref, segr_ref, dq_ref, dk_ref, dv_ref, dk_acc, dv_acc):
    length = q_ref.shape[0]
    q_low, k_low, v_low, g_low = q_ref[...], k_ref[...], v_ref[...], g_ref[...]
    lane = lax.broadcasted_iota(jnp.int32, (1, PAIR), 1)
    k_t = k_low.T
    zero = jnp.zeros((), BF16)
    cosine, slo, shi = cos_ref[...], slo_ref[...], shi_ref[...]
    first = lane < HEAD_DIM
    count = length // blk
    for b in reversed(range(count)):
        rows = slice(b * blk, (b + 1) * blk)
        keys = (b + 1) * blk
        mask = allowed_mask(segc_ref[:keys, :1], segr_ref[:1, rows], 0, keys, b * blk, blk)
        dq_t, dk_h, dv_h = [], [], []
        for h in range(2):
            mine = first if h == 0 else jnp.logical_not(first)
            qh = jnp.where(mine, q_low[rows], zero)
            gh = jnp.where(mine, g_low[rows], zero)
            s = jnp.where(mask, nt(k_low[:keys], qh), NEG)
            p = jnp.exp(s - lse_ref[0, h : h + 1, rows])
            dp = nt(v_low[:keys], gh)
            delta = jnp.sum(p * dp, axis=0, keepdims=True)
            ds = (p * (dp - delta)).astype(BF16)
            dq_t.append(nn(k_t[h * HEAD_DIM : (h + 1) * HEAD_DIM, :keys], ds))
            dk_h.append(nn(ds, q_low[rows]))
            dv_h.append(nn(p.astype(BF16), g_low[rows]))
        dk_new = jnp.where(first, dk_h[0], dk_h[1])
        dv_new = jnp.where(first, dv_h[0], dv_h[1])
        if b == count - 1:
            dk_acc[...] = dk_new
            dv_acc[...] = dv_new
        else:
            dk_acc[:keys] += dk_new
            dv_acc[:keys] += dv_new
        dq = jnp.concatenate(dq_t, 0).T * (HEAD_DIM**-0.5)
        dq_ref[rows, :] = rotate_pair(dq, cosine[rows], -slo[rows], -shi[rows]).astype(BF16)
    dk_ref[...] = rotate_pair(dk_acc[...], cosine, -slo, -shi).astype(BF16)
    dv_ref[...] = dv_acc[...].astype(BF16)


def attend_back(q, k, v, g, lse, tables, seg_col, seg_row, blk):
    length, heads_wide = q.shape
    pairs = heads_wide // PAIR
    col = pl.BlockSpec((length, PAIR), lambda p: (0, p))
    fixed = lambda shape: pl.BlockSpec(shape, lambda p: (0, 0))
    return pl.pallas_call(
        functools.partial(attend_back_kernel, blk),
        grid=(pairs,),
        in_specs=[col] * 4
        + [pl.BlockSpec((1, 2, length), lambda p: (p, 0, 0))]
        + [fixed((length, PAIR))] * 3
        + [fixed((length, 1)), fixed((1, length))],
        out_specs=[col] * 3,
        out_shape=[jax.ShapeDtypeStruct((length, heads_wide), BF16)] * 3,
        scratch_shapes=[pltpu.VMEM((length, PAIR), F32)] * 2,
        compiler_params=pltpu.CompilerParams(vmem_limit_bytes=56 << 20),
        name="attend_back",
    )(q, k, v, g, lse, *tables, seg_col, seg_row)


def pick(x, index, axis=0):
    return lax.dynamic_index_in_dim(x, index, axis, keepdims=False)


def shift(x, offset, count):
    return lax.ppermute(x, "shard", [(i, (i + offset) % count) for i in range(count)])


def gather_row(x, count, me):
    half = x.shape[0] // 2
    out = jnp.zeros((count,) + x.shape, x.dtype)
    out = lax.dynamic_update_slice(out, x[None], (me, 0, 0))
    fore = aft = x
    for step in range(1, count // 2):
        fore = shift(fore, 1, count)
        aft = shift(aft, -1, count)
        out = lax.dynamic_update_slice(out, fore[None], ((me - step) % count, 0, 0))
        out = lax.dynamic_update_slice(out, aft[None], ((me + step) % count, 0, 0))
    far = (me + count // 2) % count
    fore = shift(fore[:half], 1, count)
    aft = shift(aft[half:], -1, count)
    out = lax.dynamic_update_slice(out, fore[None], (far, 0, 0))
    out = lax.dynamic_update_slice(out, aft[None], (far, half, 0))
    return out.reshape(count * x.shape[0], x.shape[1])


def scatter_row(x, count, me):
    x = x.reshape(count, x.shape[0] // count, x.shape[1])
    half = x.shape[1] // 2

    def block(step):
        return pick(x, (me + step) % count)

    far = block(count // 2)
    fore = shift(far[:half], 1, count)
    aft = shift(far[half:], -1, count)
    for step in range(count // 2 - 1, 0, -1):
        ahead, behind = block(step).astype(F32), block(-step).astype(F32)
        if fore.shape[0] == half:
            ahead = jnp.concatenate([ahead[:half] + fore.astype(F32), ahead[half:]], 0)
            behind = jnp.concatenate([behind[:half], behind[half:] + aft.astype(F32)], 0)
        else:
            ahead = ahead + fore.astype(F32)
            behind = behind + aft.astype(F32)
        fore = shift(ahead.astype(BF16), 1, count)
        aft = shift(behind.astype(BF16), -1, count)
    return block(0).astype(F32) + fore.astype(F32) + aft.astype(F32)


def scatter_direct(x, count, me):
    x = x.reshape(count, x.shape[0] // count, x.shape[1])
    out = pick(x, me).astype(F32)
    for step in range(1, count):
        out = out + shift(pick(x, (me + step) % count), step, count).astype(F32)
    return out


def gather_small(x, count, me):
    out = lax.dynamic_update_slice(jnp.zeros((count,) + x.shape, x.dtype), x[None], (me, 0))
    for step in range(1, count):
        out = lax.dynamic_update_slice(out, shift(x, step, count)[None], ((me - step) % count, 0))
    return out


def swap_blocks(x, axis, count, me):
    out = jnp.zeros(x.shape, x.dtype)

    def put(out, block, place):
        start = [0] * x.ndim
        start[axis] = place
        return lax.dynamic_update_slice(out, jnp.expand_dims(block, axis), start)

    out = put(out, pick(x, me, axis), me)
    for step in range(1, count):
        block = shift(pick(x, (me + step) % count, axis), step, count)
        out = put(out, block, (me - step) % count)
    return out


def flip(x, mask, reps):
    return lax.ppermute(x, "rep", [(i, i ^ mask) for i in range(reps)])


def reduce_chips(x, rep, reps):
    lead, rows, cols = x.shape
    chips = reps // 2
    x = x.reshape(lead, chips, rows // chips, cols)
    mine = rep >> 1
    arrived = [flip(pick(x, mine ^ mask, 1), 2 * mask, reps) for mask in range(1, chips)]

    def total():
        out = pick(x, mine, 1).astype(F32)
        for term in arrived:
            out = out + term.astype(F32)
        return out.astype(BF16)

    return total


def spread(x, reps):
    own = [x] + [flip(x, 2 * mask, reps) for mask in range(1, reps // 2)]
    return own + [flip(piece, 1, reps) for piece in own]


def assemble(pieces, rep, wide):
    chips = len(pieces) // 2
    lead, rows, cols = pieces[0].shape
    tile = max(8, rows // 2)
    tiles = rows // tile
    groups, width = (1, 2 * cols * lead) if wide else (lead, 2 * cols)

    def kernel(place_ref, *refs):
        out = refs[-1]
        for i in range(chips):

            @pl.when(pl.program_id(0) == i)
            def _(i=i):
                for side, ref in ((place_ref[1], refs[i]), (1 - place_ref[1], refs[chips + i])):
                    for l in range(lead):
                        at = pl.multiple_of(side * cols + (l * 2 * cols if wide else 0), 128)
                        out[0 if wide else l, 0, :, pl.ds(at, cols)] = ref[l].astype(F32)

    def source(i):
        return pl.BlockSpec(
            (lead, tile, cols),
            lambda p, t, place: (0, jnp.where(p == i, t, jnp.where(p < i, 0, tiles - 1)), 0),
        )

    out = pl.pallas_call(
        kernel,
        grid_spec=pltpu.PrefetchScalarGridSpec(
            num_scalar_prefetch=1,
            grid=(chips, tiles),
            in_specs=[source(i) for i in range(chips)] * 2,
            out_specs=pl.BlockSpec(
                (groups, 1, tile, width), lambda p, t, place: (0, place[0] ^ p, t, 0)
            ),
        ),
        out_shape=jax.ShapeDtypeStruct((groups, chips, rows, width), F32),
        compiler_params=pltpu.CompilerParams(vmem_limit_bytes=48 << 20),
        name="assemble",
    )(jnp.stack([rep >> 1, rep & 1]), *pieces)
    return out.reshape(groups * chips * rows, width)


def hold(*xs):
    return lax.optimization_barrier(xs)


def local(
    tokens,
    segments,
    positions,
    norm_gain,
    norm_shift,
    inproj_weight,
    inproj_bias,
    outproj_weight,
    outproj_bias,
    expand_weight,
    expand_bias,
    shrink_weight,
    shrink_bias,
    out_grad,
):
    span, width = tokens.shape[1:]
    count = lax.axis_size("shard")
    reps = lax.axis_size("rep")
    bits = reps.bit_length() - 1
    me = lax.axis_index("shard")
    rep = lax.axis_index("rep")
    core = rep & 1
    length = span * count
    part = width // count
    inner = expand_weight.shape[0]
    sub = part // reps

    kind_of = np.zeros((count, 3), np.int32)
    forward = [[(s, (3 * s + j) % count) for s in range(count)] for j in range(3)]
    for s in range(count):
        for j in range(3):
            kind_of[(3 * s + j) % count, j] = (3 * s + j) // count
    round_of = np.argsort(kind_of, 1).astype(np.int32)

    down = jnp.concatenate(
        [
            lax.dynamic_slice_in_dim(shrink_weight, rep * sub, sub, 0).reshape(sub, count, inner),
            lax.dynamic_slice_in_dim(outproj_weight, rep * sub, sub, 0).reshape(sub, count, part),
        ],
        2,
    )
    down = swap_blocks(jnp.transpose(down, (1, 0, 2)), 0, count, me)

    packed = jnp.concatenate([norm_gain, norm_shift, outproj_bias, shrink_bias, inproj_bias])
    packed = gather_small(packed, count, me)
    gain, shift_all, outbias, shrbias = (
        packed[:, i * part : (i + 1) * part].reshape(width).astype(F32) for i in range(4)
    )
    inbias = packed[:, 4 * part :].reshape(3, count, part)
    inbias = pick(inbias, me, 1).reshape(3 * part).astype(F32)

    grad_own = out_grad.reshape(span, width)
    grads = gather_row(grad_own, count, me)

    residual = tokens.reshape(span, width).astype(F32)
    row_mean = jnp.mean(residual, -1, keepdims=True)
    centered = residual - row_mean
    row_var = jnp.mean(centered * centered, -1, keepdims=True)
    inv_std = lax.rsqrt(row_var + 1e-05)
    xhat = centered * inv_std
    normed_own = (xhat * gain + shift_all).astype(BF16)
    normed = gather_row(normed_own, count, me)

    down = lax.all_gather(down, "rep", axis=1, tiled=True).reshape(width, inner + part)
    shrink_w, out_w = down[:, :inner], down[:, inner:]

    seg = segments.reshape(length)
    starts = jnp.sum((seg[None, :] < seg[:, None]).astype(jnp.int32), 1)
    place = (jnp.arange(length, dtype=jnp.int32) - starts).astype(F32)
    inverse_freq = 10000.0 ** (-jnp.arange(ROT // 2).astype(F32) * 2.0 / ROT)
    angle = place[:, None] * inverse_freq[None, :]
    cosine, sine = jnp.cos(angle), jnp.sin(angle)
    quiet = jnp.zeros_like(sine)
    rest = jnp.zeros((length, HEAD_DIM - ROT), F32)
    tables = (
        jnp.concatenate([cosine, cosine, rest + 1.0] * 2, 1),
        jnp.concatenate([-sine, quiet, rest] * 2, 1),
        jnp.concatenate([quiet, sine, rest] * 2, 1),
    )
    seg_col, seg_row = seg[:, None], seg[None, :]
    blk = min(256, length)
    back = [[(b, a) for a, b in pairs] for pairs in forward]

    def col_half(x, which):
        wide = x.shape[1] // 2
        return lax.dynamic_slice_in_dim(x, which * wide, wide, 1)

    def low_term(outputs, inputs, extra=None):
        out = tn(outputs, inputs)
        return (out if extra is None else out + extra.astype(F32)).astype(BF16)

    normed_mine, normed_other = col_half(normed, core), col_half(normed, 1 - core)
    expanded = nt(normed, expand_weight) + expand_bias.astype(F32)
    hidden, slope = gelu_parts(expanded)
    hidden = hidden.astype(BF16)
    hidden_mine, hidden_other = col_half(hidden, core), col_half(hidden, 1 - core)

    slices = lax.dynamic_slice_in_dim(inproj_weight.reshape(3, part, width), rep * sub, sub, 1)
    grads, slices = hold(grads, slices)
    arrived = jnp.stack([lax.ppermute(slices[j], "shard", forward[j]) for j in range(3)])
    my_rounds = pick(jnp.asarray(round_of), me)
    arrived = jnp.stack([pick(arrived, my_rounds[k]) for k in range(3)])
    in_w = lax.all_gather(arrived, "rep", axis=1, tiled=True).reshape(3 * part, width)

    blocks = inner // part
    shr_send = low_term(grads, hidden_other)
    shr_arrived = flip(shr_send, 1, reps)
    grads_1, shr_send = hold(grads, shr_send)
    d_up = (nn(grads_1, shrink_w) * slope).astype(BF16)
    grads_2, d_up = hold(grads_1, d_up)
    shr_sum = low_term(grads_2, hidden_mine, shr_arrived)
    shr_total = reduce_chips(shr_sum.reshape(count, part, inner // 2), rep, reps)
    d_up, shr_sum = hold(d_up, shr_sum)
    exp_send = low_term(d_up, normed_other)
    exp_arrived = flip(exp_send, 1, reps)
    grads_3, exp_send = hold(grads_2, exp_send)
    d_att = nn(grads_3, out_w).astype(BF16)
    d_up_1, d_att = hold(d_up, d_att)
    exp_sum = low_term(d_up_1, normed_mine, exp_arrived)
    exp_total = reduce_chips(exp_sum.reshape(blocks, part, width // 2), rep, reps)

    normed_1, exp_sum = hold(normed, exp_sum)
    mixed = nt(normed_1, in_w) + inbias
    attended, q_low, k_low, v_low, lse = attend(mixed, tables, seg_col, seg_row, blk)
    grads_4, attended = hold(grads_3, attended)
    g_out = tn(grads_4, attended).astype(BF16)
    hidden_1, g_out = hold(hidden, g_out)
    g_out = lax.psum_scatter(
        g_out.reshape(count, part, part), "rep", scatter_dimension=1, tiled=True
    )
    g_shr = shr_total()
    g_shr = swap_blocks(g_shr, 0, count, me)
    branches = (nt(hidden_1, shrink_w) + nt(attended, out_w)).astype(BF16)
    branches_sum = scatter_direct(branches, count, me)
    shr_pieces = spread(g_shr, reps)
    g_exp = exp_total()
    exp_pieces = spread(g_exp, reps)

    d_att, branches, g_exp = hold(d_att, branches, g_exp)
    d_q, d_k, d_v = attend_back(q_low, k_low, v_low, d_att, lse, tables, seg_col, seg_row, blk)
    d_mixed = jnp.concatenate([d_q, d_k, d_v], 1)
    g_out, d_mixed = hold(g_out, d_mixed)
    in_send = low_term(d_mixed, normed_other)
    in_arrived = flip(in_send, 1, reps)
    g_out = jnp.transpose(swap_blocks(g_out, 0, count, me), (1, 0, 2)).reshape(sub, width)
    in_sum = low_term(d_mixed, normed_mine, in_arrived)
    in_total = reduce_chips(in_sum.reshape(3, part, width // 2), rep, reps)
    d_up_3, in_sum = hold(d_up_1, in_sum)
    d_normed = (nn(d_up_3, expand_weight) + nn(d_mixed, in_w)).astype(BF16)
    d_normed = scatter_row(d_normed, count, me)
    g_out = lax.all_gather(g_out, "rep", axis=0, tiled=True).astype(F32)

    g_shr = assemble(shr_pieces, rep, True)
    kinds = pick(jnp.asarray(kind_of), me)
    g_in = in_total()
    g_in = jnp.stack([lax.ppermute(pick(g_in, kinds[j]), "shard", back[j]) for j in range(3)])
    in_pieces = spread(g_in, reps)
    g_exp = assemble(exp_pieces, rep, False)
    g_in = assemble(in_pieces, rep, False)
    block_output = (residual + (branches_sum + (outbias + shrbias))).astype(BF16)

    d_hat = d_normed * gain
    token_grad = grad_own.astype(F32) + inv_std * (
        d_hat
        - jnp.mean(d_hat, -1, keepdims=True)
        - xhat * jnp.mean(d_hat * xhat, -1, keepdims=True)
    )

    b_out = jnp.sum(lax.dynamic_slice_in_dim(grads, me * part, part, 1), 0, dtype=F32)
    b_exp = jnp.sum(d_up, 0, dtype=F32)
    b_in = jnp.sum(d_mixed, 0, dtype=F32)
    sums = jnp.concatenate([b_out, b_exp, b_in])
    for bit in range(bits):
        sums = sums + flip(sums, 1 << bit, reps)
    b_out, b_exp, b_in = sums[:part], sums[part : part + inner], sums[part + inner :]
    b_in = b_in.reshape(3, part)
    b_in = jnp.concatenate([lax.ppermute(pick(b_in, kinds[j]), "shard", back[j]) for j in range(3)])
    both = jnp.stack([jnp.sum(d_normed * xhat, 0), jnp.sum(d_normed, 0)])
    both = jnp.sum(swap_blocks(both.reshape(2, count, part), 1, count, me), 1)
    for bit in range(bits):
        both = both + flip(both, 1 << bit, reps)

    return (
        block_output[None],
        token_grad[None],
        both[0],
        both[1],
        g_in,
        b_in,
        g_out,
        b_out,
        g_exp,
        b_exp,
        g_shr,
        b_out,
    )


def solution(mesh):
    in_specs = (
        P("rep", "shard", None),
        P("rep", None),
        P("rep", "shard"),
        P("shard"),
        P("shard"),
        P("shard", None),
        P("shard"),
        P("shard", None),
        P("shard"),
        P("shard", None),
        P("shard"),
        P("shard", None),
        P("shard"),
        P("rep", "shard", None),
    )
    out_specs = (
        P("rep", "shard", None),
        P("rep", "shard", None),
        P("shard"),
        P("shard"),
        P("shard", None),
        P("shard"),
        P("shard", None),
        P("shard"),
        P("shard", None),
        P("shard"),
        P("shard", None),
        P("shard"),
    )

    return jax.shard_map(local, mesh=mesh, in_specs=in_specs, out_specs=out_specs, check_vma=False)
```

```python
import functools
import math

import jax
import jax.numpy as jnp
import numpy as np
from jax import lax
from jax.experimental import pallas as pl
from jax.experimental.pallas import tpu as pltpu
from jax.sharding import PartitionSpec as P


HEAD_DIM = 64
ROT = 32
PAIR = 2 * HEAD_DIM
NEG = -1e30
F32 = jnp.float32
BF16 = jnp.bfloat16


def nt(a, b):
    return lax.dot_general(a, b, (((1,), (1,)), ((), ())), preferred_element_type=F32)


def nn(a, b):
    return lax.dot_general(a, b, (((1,), (0,)), ((), ())), preferred_element_type=F32)


def tn(a, b):
    return lax.dot_general(a, b, (((0,), (0,)), ((), ())), preferred_element_type=F32)


def gelu_parts(values):
    c = math.sqrt(2.0 / math.pi)
    square = values * values
    t = jnp.tanh(c * (values + 0.044715 * square * values))
    half = 0.5 * (1.0 + t)
    slope = half + 0.5 * values * (1.0 - t * t) * (c * (1.0 + 3.0 * 0.044715 * square))
    return values * half, slope


def rotate_pair(x, cosine, sine_low, sine_high):
    quarter = ROT // 2
    up = pltpu.roll(x, PAIR - quarter, 1)
    down = pltpu.roll(x, quarter, 1)
    return x * cosine + up * sine_low + down * sine_high


def allowed_mask(seg_col, seg_row, first_key, keys, first_query, queries):
    same = seg_col == seg_row
    kpos = first_key + lax.broadcasted_iota(jnp.int32, (keys, queries), 0)
    qpos = first_query + lax.broadcasted_iota(jnp.int32, (keys, queries), 1)
    return same & (kpos <= qpos)


def attend_kernel(blk, q_ref, k_ref, v_ref, cos_ref, slo_ref, shi_ref, segc_ref, segr_ref,
                  o_ref, q_out, k_out, v_out, lse_ref):
    length = q_ref.shape[0]
    cosine, slo, shi = cos_ref[...], slo_ref[...], shi_ref[...]
    q_low = (rotate_pair(q_ref[...], cosine, slo, shi).astype(BF16)) * jnp.asarray(HEAD_DIM**-0.5, BF16)
    k_low = rotate_pair(k_ref[...], cosine, slo, shi).astype(BF16)
    v_low = v_ref[...].astype(BF16)
    q_out[...] = q_low
    k_out[...] = k_low
    v_out[...] = v_low
    lane = lax.broadcasted_iota(jnp.int32, (1, PAIR), 1)
    v_t = v_low.T
    for b in range(length // blk):
        rows = slice(b * blk, (b + 1) * blk)
        keys = (b + 1) * blk
        mask = allowed_mask(segc_ref[:keys, :1], segr_ref[:1, rows], 0, keys, b * blk, blk)
        outs = []
        for h in range(2):
            mine = (lane < HEAD_DIM) if h == 0 else (lane >= HEAD_DIM)
            qh = jnp.where(mine, q_low[rows], jnp.zeros((), BF16))
            s = jnp.where(mask, nt(k_low[:keys], qh), NEG)
            top = jnp.max(s, axis=0, keepdims=True)
            e = jnp.exp(s - top)
            total = jnp.sum(e, axis=0, keepdims=True)
            p = (e * (1.0 / total)).astype(BF16)
            lse_ref[0, h : h + 1, rows] = top + jnp.log(total)
            outs.append(nn(v_t[h * HEAD_DIM : (h + 1) * HEAD_DIM, :keys], p))
        o_ref[rows, :] = jnp.concatenate(outs, 0).T.astype(BF16)


def attend(mixed, tables, seg_col, seg_row, blk):
    length, wide = mixed.shape
    heads_wide = wide // 3
    pairs = heads_wide // PAIR
    col = lambda off: pl.BlockSpec((length, PAIR), lambda p: (0, off + p))
    fixed = lambda shape: pl.BlockSpec(shape, lambda p: (0, 0))
    return pl.pallas_call(
        functools.partial(attend_kernel, blk),
        grid=(pairs,),
        in_specs=[col(0), col(pairs), col(2 * pairs)]
        + [fixed((length, PAIR))] * 3
        + [fixed((length, 1)), fixed((1, length))],
        out_specs=[col(0)] * 4 + [pl.BlockSpec((1, 2, length), lambda p: (p, 0, 0))],
        out_shape=[jax.ShapeDtypeStruct((length, heads_wide), BF16)] * 4
        + [jax.ShapeDtypeStruct((pairs, 2, length), F32)],
        compiler_params=pltpu.CompilerParams(vmem_limit_bytes=56 << 20),
        name="attend",
    )(mixed, mixed, mixed, *tables, seg_col, seg_row)


def attend_back_kernel(blk, q_ref, k_ref, v_ref, g_ref, lse_ref, cos_ref, slo_ref, shi_ref,
                       segc_ref, segr_ref, dq_ref, dk_ref, dv_ref, dk_acc, dv_acc):
    length = q_ref.shape[0]
    q_low, k_low, v_low, g_low = q_ref[...], k_ref[...], v_ref[...], g_ref[...]
    lane = lax.broadcasted_iota(jnp.int32, (1, PAIR), 1)
    k_t = k_low.T
    zero = jnp.zeros((), BF16)
    cosine, slo, shi = cos_ref[...], slo_ref[...], shi_ref[...]
    first = lane < HEAD_DIM
    count = length // blk
    for b in reversed(range(count)):
        rows = slice(b * blk, (b + 1) * blk)
        keys = (b + 1) * blk
        mask = allowed_mask(segc_ref[:keys, :1], segr_ref[:1, rows], 0, keys, b * blk, blk)
        dq_t, dk_h, dv_h = [], [], []
        for h in range(2):
            mine = first if h == 0 else jnp.logical_not(first)
            qh = jnp.where(mine, q_low[rows], zero)
            gh = jnp.where(mine, g_low[rows], zero)
            s = jnp.where(mask, nt(k_low[:keys], qh), NEG)
            p = jnp.exp(s - lse_ref[0, h : h + 1, rows])
            dp = nt(v_low[:keys], gh)
            delta = jnp.sum(p * dp, axis=0, keepdims=True)
            ds = (p * (dp - delta)).astype(BF16)
            dq_t.append(nn(k_t[h * HEAD_DIM : (h + 1) * HEAD_DIM, :keys], ds))
            dk_h.append(nn(ds, q_low[rows]))
            dv_h.append(nn(p.astype(BF16), g_low[rows]))
        dk_new = jnp.where(first, dk_h[0], dk_h[1])
        dv_new = jnp.where(first, dv_h[0], dv_h[1])
        if b == count - 1:
            dk_acc[...] = dk_new
            dv_acc[...] = dv_new
        else:
            dk_acc[:keys] += dk_new
            dv_acc[:keys] += dv_new
        dq = jnp.concatenate(dq_t, 0).T * (HEAD_DIM**-0.5)
        dq_ref[rows, :] = rotate_pair(dq, cosine[rows], -slo[rows], -shi[rows]).astype(BF16)
    dk_ref[...] = rotate_pair(dk_acc[...], cosine, -slo, -shi).astype(BF16)
    dv_ref[...] = dv_acc[...].astype(BF16)


def attend_back(q, k, v, g, lse, tables, seg_col, seg_row, blk):
    length, heads_wide = q.shape
    pairs = heads_wide // PAIR
    col = pl.BlockSpec((length, PAIR), lambda p: (0, p))
    fixed = lambda shape: pl.BlockSpec(shape, lambda p: (0, 0))
    return pl.pallas_call(
        functools.partial(attend_back_kernel, blk),
        grid=(pairs,),
        in_specs=[col] * 4
        + [pl.BlockSpec((1, 2, length), lambda p: (p, 0, 0))]
        + [fixed((length, PAIR))] * 3
        + [fixed((length, 1)), fixed((1, length))],
        out_specs=[col] * 3,
        out_shape=[jax.ShapeDtypeStruct((length, heads_wide), BF16)] * 3,
        scratch_shapes=[pltpu.VMEM((length, PAIR), F32)] * 2,
        compiler_params=pltpu.CompilerParams(vmem_limit_bytes=56 << 20),
        name="attend_back",
    )(q, k, v, g, lse, *tables, seg_col, seg_row)


def pick(x, index, axis=0):
    return lax.dynamic_index_in_dim(x, index, axis, keepdims=False)


def shift(x, offset, count):
    return lax.ppermute(x, "shard", [(i, (i + offset) % count) for i in range(count)])


def gather_row(x, count, me):
    half = x.shape[0] // 2
    out = jnp.zeros((count,) + x.shape, x.dtype)
    out = lax.dynamic_update_slice(out, x[None], (me, 0, 0))
    fore = aft = x
    for step in range(1, count // 2):
        fore = shift(fore, 1, count)
        aft = shift(aft, -1, count)
        out = lax.dynamic_update_slice(out, fore[None], ((me - step) % count, 0, 0))
        out = lax.dynamic_update_slice(out, aft[None], ((me + step) % count, 0, 0))
    far = (me + count // 2) % count
    fore = shift(fore[:half], 1, count)
    aft = shift(aft[half:], -1, count)
    out = lax.dynamic_update_slice(out, fore[None], (far, 0, 0))
    out = lax.dynamic_update_slice(out, aft[None], (far, half, 0))
    return out.reshape(count * x.shape[0], x.shape[1])


def scatter_row(x, count, me):
    x = x.reshape(count, x.shape[0] // count, x.shape[1])
    half = x.shape[1] // 2

    def block(step):
        return pick(x, (me + step) % count)

    far = block(count // 2)
    fore = shift(far[:half], 1, count)
    aft = shift(far[half:], -1, count)
    for step in range(count // 2 - 1, 0, -1):
        ahead, behind = block(step).astype(F32), block(-step).astype(F32)
        if fore.shape[0] == half:
            ahead = jnp.concatenate([ahead[:half] + fore.astype(F32), ahead[half:]], 0)
            behind = jnp.concatenate([behind[:half], behind[half:] + aft.astype(F32)], 0)
        else:
            ahead = ahead + fore.astype(F32)
            behind = behind + aft.astype(F32)
        fore = shift(ahead.astype(BF16), 1, count)
        aft = shift(behind.astype(BF16), -1, count)
    return block(0).astype(F32) + fore.astype(F32) + aft.astype(F32)


def scatter_direct(x, count, me):
    x = x.reshape(count, x.shape[0] // count, x.shape[1])
    out = pick(x, me).astype(F32)
    for step in range(1, count):
        out = out + shift(pick(x, (me + step) % count), step, count).astype(F32)
    return out


def gather_small(x, count, me):
    out = lax.dynamic_update_slice(jnp.zeros((count,) + x.shape, x.dtype), x[None], (me, 0))
    for step in range(1, count):
        out = lax.dynamic_update_slice(out, shift(x, step, count)[None], ((me - step) % count, 0))
    return out


def swap_blocks(x, axis, count, me):
    out = jnp.zeros(x.shape, x.dtype)

    def put(out, block, place):
        start = [0] * x.ndim
        start[axis] = place
        return lax.dynamic_update_slice(out, jnp.expand_dims(block, axis), start)

    out = put(out, pick(x, me, axis), me)
    for step in range(1, count):
        block = shift(pick(x, (me + step) % count, axis), step, count)
        out = put(out, block, (me - step) % count)
    return out


def flip(x, mask, reps):
    return lax.ppermute(x, "rep", [(i, i ^ mask) for i in range(reps)])


def reduce_chips(x, rep, reps):
    lead, rows, cols = x.shape
    chips = reps // 2
    x = x.reshape(lead, chips, rows // chips, cols)
    mine = rep >> 1
    arrived = [flip(pick(x, mine ^ mask, 1), 2 * mask, reps) for mask in range(1, chips)]

    def total():
        out = pick(x, mine, 1).astype(F32)
        for term in arrived:
            out = out + term.astype(F32)
        return out.astype(BF16)

    return total


def spread(x, reps):
    own = [x] + [flip(x, 2 * mask, reps) for mask in range(1, reps // 2)]
    return own + [flip(piece, 1, reps) for piece in own]


def assemble(pieces, rep, wide):
    chips = len(pieces) // 2
    lead, rows, cols = pieces[0].shape
    tile = max(8, rows // 2)
    tiles = rows // tile
    groups, width = (1, 2 * cols * lead) if wide else (lead, 2 * cols)

    def kernel(place_ref, *refs):
        out = refs[-1]
        for i in range(chips):

            @pl.when(pl.program_id(0) == i)
            def _(i=i):
                for side, ref in ((place_ref[1], refs[i]), (1 - place_ref[1], refs[chips + i])):
                    for l in range(lead):
                        at = pl.multiple_of(side * cols + (l * 2 * cols if wide else 0), 128)
                        out[0 if wide else l, 0, :, pl.ds(at, cols)] = ref[l].astype(F32)

    def source(i):
        return pl.BlockSpec(
            (lead, tile, cols),
            lambda p, t, place: (0, jnp.where(p == i, t, jnp.where(p < i, 0, tiles - 1)), 0),
        )

    out = pl.pallas_call(
        kernel,
        grid_spec=pltpu.PrefetchScalarGridSpec(
            num_scalar_prefetch=1,
            grid=(chips, tiles),
            in_specs=[source(i) for i in range(chips)] * 2,
            out_specs=pl.BlockSpec(
                (groups, 1, tile, width), lambda p, t, place: (0, place[0] ^ p, t, 0)
            ),
        ),
        out_shape=jax.ShapeDtypeStruct((groups, chips, rows, width), F32),
        compiler_params=pltpu.CompilerParams(vmem_limit_bytes=48 << 20),
        name="assemble",
    )(jnp.stack([rep >> 1, rep & 1]), *pieces)
    return out.reshape(groups * chips * rows, width)


def lay_out(x, wide):
    reps, lead, rows, cols = x.shape
    tile = max(8, rows // 2)
    groups, width = (1, 2 * cols * lead) if wide else (lead, 2 * cols)

    def kernel(x_ref, out):
        for side in range(2):
            for l in range(lead):
                at = side * cols + (l * 2 * cols if wide else 0)
                out[0 if wide else l, 0, :, at : at + cols] = x_ref[side, l].astype(F32)

    out = pl.pallas_call(
        kernel,
        grid=(reps // 2, rows // tile),
        in_specs=[pl.BlockSpec((2, lead, tile, cols), lambda p, t: (p, 0, t, 0))],
        out_specs=pl.BlockSpec((groups, 1, tile, width), lambda p, t: (0, p, t, 0)),
        out_shape=jax.ShapeDtypeStruct((groups, reps // 2, rows, width), F32),
        compiler_params=pltpu.CompilerParams(vmem_limit_bytes=48 << 20),
        name="place",
    )(x)
    return out.reshape(groups * (reps // 2) * rows, width)


def hold(*xs):
    return lax.optimization_barrier(xs)


def local(
    tokens,
    segments,
    positions,
    norm_gain,
    norm_shift,
    inproj_weight,
    inproj_bias,
    outproj_weight,
    outproj_bias,
    expand_weight,
    expand_bias,
    shrink_weight,
    shrink_bias,
    out_grad,
):
    span, width = tokens.shape[1:]
    count = lax.axis_size("shard")
    reps = lax.axis_size("rep")
    bits = reps.bit_length() - 1
    me = lax.axis_index("shard")
    rep = lax.axis_index("rep")
    core = rep & 1
    length = span * count
    part = width // count
    inner = expand_weight.shape[0]
    sub = part // reps

    kind_of = np.zeros((count, 3), np.int32)
    forward = [[(s, (3 * s + j) % count) for s in range(count)] for j in range(3)]
    for s in range(count):
        for j in range(3):
            kind_of[(3 * s + j) % count, j] = (3 * s + j) // count
    round_of = np.argsort(kind_of, 1).astype(np.int32)

    packed = jnp.concatenate([norm_gain, norm_shift, outproj_bias, shrink_bias, inproj_bias])
    packed = gather_small(packed, count, me)
    gain, shift_all, outbias, shrbias = (
        packed[:, i * part : (i + 1) * part].reshape(width).astype(F32) for i in range(4)
    )
    inbias = packed[:, 4 * part :].reshape(3, count, part)
    inbias = pick(inbias, me, 1).reshape(3 * part).astype(F32)

    slices = lax.dynamic_slice_in_dim(inproj_weight.reshape(3, part, width), rep * sub, sub, 1)
    arrived = jnp.stack([lax.ppermute(slices[j], "shard", forward[j]) for j in range(3)])
    my_rounds = pick(jnp.asarray(round_of), me)
    arrived = jnp.stack([pick(arrived, my_rounds[k]) for k in range(3)])
    in_w = lax.all_gather(arrived, "rep", axis=1, tiled=True).reshape(3 * part, width)

    grad_own = out_grad.reshape(span, width)
    grads = gather_row(grad_own, count, me)

    residual = tokens.reshape(span, width).astype(F32)
    row_mean = jnp.mean(residual, -1, keepdims=True)
    centered = residual - row_mean
    row_var = jnp.mean(centered * centered, -1, keepdims=True)
    inv_std = lax.rsqrt(row_var + 1e-05)
    xhat = centered * inv_std
    normed_own = (xhat * gain + shift_all).astype(BF16)
    normed = gather_row(normed_own, count, me)

    seg = segments.reshape(length)
    starts = jnp.sum((seg[None, :] < seg[:, None]).astype(jnp.int32), 1)
    place = (jnp.arange(length, dtype=jnp.int32) - starts).astype(F32)
    inverse_freq = 10000.0 ** (-jnp.arange(ROT // 2).astype(F32) * 2.0 / ROT)
    angle = place[:, None] * inverse_freq[None, :]
    cosine, sine = jnp.cos(angle), jnp.sin(angle)
    quiet = jnp.zeros_like(sine)
    rest = jnp.zeros((length, HEAD_DIM - ROT), F32)
    tables = (
        jnp.concatenate([cosine, cosine, rest + 1.0] * 2, 1),
        jnp.concatenate([-sine, quiet, rest] * 2, 1),
        jnp.concatenate([quiet, sine, rest] * 2, 1),
    )
    seg_col, seg_row = seg[:, None], seg[None, :]
    blk = min(256, length)
    back = [[(b, a) for a, b in pairs] for pairs in forward]

    down = jnp.concatenate(
        [
            lax.dynamic_slice_in_dim(shrink_weight, rep * sub, sub, 0).reshape(sub, count, inner),
            lax.dynamic_slice_in_dim(outproj_weight, rep * sub, sub, 0).reshape(sub, count, part),
        ],
        2,
    )
    down = jnp.transpose(down, (1, 0, 2))
    grads, down = hold(grads, down)
    down = swap_blocks(down, 0, count, me)
    shrink_w = lax.all_gather(down[:, :, :inner], "rep", axis=1, tiled=True).reshape(width, inner)
    out_w = lax.all_gather(down[:, :, inner:], "rep", axis=1, tiled=True).reshape(width, part)

    def col_half(x, which):
        wide = x.shape[1] // 2
        return lax.dynamic_slice_in_dim(x, which * wide, wide, 1)

    def low_term(outputs, inputs, extra=None):
        out = tn(outputs, inputs)
        return (out if extra is None else out + extra.astype(F32)).astype(BF16)

    normed_mine, normed_other = col_half(normed, core), col_half(normed, 1 - core)
    expanded = nt(normed, expand_weight) + expand_bias.astype(F32)
    hidden, slope = gelu_parts(expanded)
    hidden, slope = hidden.astype(BF16), slope.astype(BF16)
    hidden_mine, hidden_other = col_half(hidden, core), col_half(hidden, 1 - core)
    shr_send = low_term(grads, hidden_other)
    shr_arrived = flip(shr_send, 1, reps)

    normed_1, shr_send = hold(normed, shr_send)
    mixed = nt(normed_1, in_w) + inbias
    grads_1, mixed = hold(grads, mixed)
    shr_sum = low_term(grads_1, hidden_mine, shr_arrived)
    shr_total = reduce_chips(shr_sum.reshape(count, part, inner // 2), rep, reps)
    mixed, shr_sum = hold(mixed, shr_sum)
    attended, q_low, k_low, v_low, lse = attend(mixed, tables, seg_col, seg_row, blk)
    grads_2, attended = hold(grads_1, attended)
    g_out = tn(grads_2, attended).astype(BF16)
    g_out_1 = lax.psum_scatter(
        g_out.reshape(count, part, part), "rep", scatter_dimension=1, tiled=True
    )
    blocks = inner // part
    grads_3, g_out = hold(grads_2, g_out)
    d_up = (nn(grads_3, shrink_w) * slope.astype(F32)).astype(BF16)
    exp_send = low_term(d_up, normed_other)
    exp_arrived = flip(exp_send, 1, reps)
    hidden_1, exp_send = hold(hidden, exp_send)
    branches = (nt(hidden_1, shrink_w) + nt(attended, out_w)).astype(BF16)
    branches_sum = scatter_direct(branches, count, me)
    d_up_1, branches = hold(d_up, branches)
    exp_sum = low_term(d_up_1, normed_mine, exp_arrived)
    exp_total = reduce_chips(exp_sum.reshape(blocks, part, width // 2), rep, reps)
    g_shr = shr_total()
    g_shr = swap_blocks(g_shr, 0, count, me)
    g_shr = lax.all_gather(g_shr, "rep", axis=0)
    grads_4, exp_sum = hold(grads_3, exp_sum)
    d_att = nn(grads_4, out_w).astype(BF16)

    d_q, d_k, d_v = attend_back(q_low, k_low, v_low, d_att, lse, tables, seg_col, seg_row, blk)
    d_mixed = jnp.concatenate([d_q, d_k, d_v], 1)
    in_send = low_term(d_mixed, normed_other)
    in_arrived = flip(in_send, 1, reps)
    g_exp = exp_total()
    exp_pieces = spread(g_exp, reps)
    d_mixed_1, in_send, g_exp = hold(d_mixed, in_send, g_exp)
    in_sum = low_term(d_mixed_1, normed_mine, in_arrived)
    in_total = reduce_chips(in_sum.reshape(3, part, width // 2), rep, reps)
    d_mixed_2, in_sum = hold(d_mixed_1, in_sum)
    d_normed = nn(d_up_1, expand_weight) + nn(d_mixed_2, in_w)
    both = jnp.stack([jnp.sum(d_normed * normed.astype(F32), 0), jnp.sum(d_normed, 0)])
    d_normed = d_normed.astype(BF16)
    g_out_1, d_normed = hold(g_out_1, d_normed)
    d_normed = scatter_row(d_normed, count, me)

    b_out = jnp.sum(lax.dynamic_slice_in_dim(grads, me * part, part, 1), 0, dtype=F32)
    b_exp = jnp.sum(d_up_1, 0, dtype=F32)
    b_in = jnp.sum(d_mixed_2, 0, dtype=F32)
    both = jnp.sum(swap_blocks(both.reshape(2, count, part), 1, count, me), 1)
    sums = jnp.concatenate([both[0], both[1], b_out, b_exp, b_in])

    kinds = pick(jnp.asarray(kind_of), me)
    g_in = in_total()
    g_in = jnp.stack([lax.ppermute(pick(g_in, kinds[j]), "shard", back[j]) for j in range(3)])
    in_pieces = spread(g_in, reps)
    g_out = jnp.transpose(swap_blocks(g_out_1, 0, count, me), (1, 0, 2)).reshape(sub, width)
    g_out = lax.all_gather(g_out, "rep", axis=0, tiled=True).astype(F32)
    g_shr = lay_out(g_shr, True)
    g_exp = assemble(exp_pieces, rep, False)
    g_in = assemble(in_pieces, rep, False)
    block_output = (residual + (branches_sum + (outbias + shrbias))).astype(BF16)

    d_hat = d_normed * gain
    token_grad = grad_own.astype(F32) + inv_std * (
        d_hat
        - jnp.mean(d_hat, -1, keepdims=True)
        - xhat * jnp.mean(d_hat * xhat, -1, keepdims=True)
    )

    for bit in range(bits):
        sums = sums + flip(sums, 1 << bit, reps)
    b_norm, b_shift, b_out = sums[:part], sums[part : 2 * part], sums[2 * part : 3 * part]
    b_gain = (b_norm - norm_shift.astype(F32) * b_shift) / norm_gain.astype(F32)
    b_exp, b_in = sums[3 * part : 3 * part + inner], sums[3 * part + inner :].reshape(3, part)
    b_in = jnp.concatenate([lax.ppermute(pick(b_in, kinds[j]), "shard", back[j]) for j in range(3)])

    return (
        block_output[None],
        token_grad[None],
        b_gain,
        b_shift,
        g_in,
        b_in,
        g_out,
        b_out,
        g_exp,
        b_exp,
        g_shr,
        b_out,
    )


def solution(mesh):
    in_specs = (
        P("rep", "shard", None),
        P("rep", None),
        P("rep", "shard"),
        P("shard"),
        P("shard"),
        P("shard", None),
        P("shard"),
        P("shard", None),
        P("shard"),
        P("shard", None),
        P("shard"),
        P("shard", None),
        P("shard"),
        P("rep", "shard", None),
    )
    out_specs = (
        P("rep", "shard", None),
        P("rep", "shard", None),
        P("shard"),
        P("shard"),
        P("shard", None),
        P("shard"),
        P("shard", None),
        P("shard"),
        P("shard", None),
        P("shard"),
        P("shard", None),
        P("shard"),
    )

    return jax.shard_map(local, mesh=mesh, in_specs=in_specs, out_specs=out_specs, check_vma=False)
```

```python
import functools
import math

import jax
import jax.numpy as jnp
import numpy as np
from jax import lax
from jax.experimental import pallas as pl
from jax.experimental.pallas import tpu as pltpu
from jax.sharding import PartitionSpec as P


HEAD_DIM = 64
ROT = 32
PAIR = 2 * HEAD_DIM
NEG = -1e30
F32 = jnp.float32
BF16 = jnp.bfloat16


def nt(a, b):
    return lax.dot_general(a, b, (((1,), (1,)), ((), ())), preferred_element_type=F32)


def nn(a, b):
    return lax.dot_general(a, b, (((1,), (0,)), ((), ())), preferred_element_type=F32)


def tn(a, b):
    return lax.dot_general(a, b, (((0,), (0,)), ((), ())), preferred_element_type=F32)


def gelu_parts(values):
    c = math.sqrt(2.0 / math.pi)
    square = values * values
    t = jnp.tanh(c * (values + 0.044715 * square * values))
    half = 0.5 * (1.0 + t)
    slope = half + 0.5 * values * (1.0 - t * t) * (c * (1.0 + 3.0 * 0.044715 * square))
    return values * half, slope


def rotate_pair(x, cosine, sine_low, sine_high):
    quarter = ROT // 2
    up = pltpu.roll(x, PAIR - quarter, 1)
    down = pltpu.roll(x, quarter, 1)
    return x * cosine + up * sine_low + down * sine_high


def allowed_mask(seg_col, seg_row, first_key, keys, first_query, queries):
    same = seg_col == seg_row
    kpos = first_key + lax.broadcasted_iota(jnp.int32, (keys, queries), 0)
    qpos = first_query + lax.broadcasted_iota(jnp.int32, (keys, queries), 1)
    return same & (kpos <= qpos)


def attend_kernel(blk, q_ref, k_ref, v_ref, cos_ref, slo_ref, shi_ref, segc_ref, segr_ref,
                  o_ref, q_out, k_out, v_out, lse_ref):
    length = q_ref.shape[0]
    cosine, slo, shi = cos_ref[...], slo_ref[...], shi_ref[...]
    q_low = (rotate_pair(q_ref[...], cosine, slo, shi).astype(BF16)) * jnp.asarray(HEAD_DIM**-0.5, BF16)
    k_low = rotate_pair(k_ref[...], cosine, slo, shi).astype(BF16)
    v_low = v_ref[...].astype(BF16)
    q_out[...] = q_low
    k_out[...] = k_low
    v_out[...] = v_low
    lane = lax.broadcasted_iota(jnp.int32, (1, PAIR), 1)
    v_t = v_low.T
    for b in range(length // blk):
        rows = slice(b * blk, (b + 1) * blk)
        keys = (b + 1) * blk
        mask = allowed_mask(segc_ref[:keys, :1], segr_ref[:1, rows], 0, keys, b * blk, blk)
        outs = []
        for h in range(2):
            mine = (lane < HEAD_DIM) if h == 0 else (lane >= HEAD_DIM)
            qh = jnp.where(mine, q_low[rows], jnp.zeros((), BF16))
            s = jnp.where(mask, nt(k_low[:keys], qh), NEG)
            top = jnp.max(s, axis=0, keepdims=True)
            e = jnp.exp(s - top)
            total = jnp.sum(e, axis=0, keepdims=True)
            p = (e * (1.0 / total)).astype(BF16)
            lse_ref[0, h : h + 1, rows] = top + jnp.log(total)
            outs.append(nn(v_t[h * HEAD_DIM : (h + 1) * HEAD_DIM, :keys], p))
        o_ref[rows, :] = jnp.concatenate(outs, 0).T.astype(BF16)


def attend(mixed, tables, seg_col, seg_row, blk):
    length, wide = mixed.shape
    heads_wide = wide // 3
    pairs = heads_wide // PAIR
    col = lambda off: pl.BlockSpec((length, PAIR), lambda p: (0, off + p))
    fixed = lambda shape: pl.BlockSpec(shape, lambda p: (0, 0))
    return pl.pallas_call(
        functools.partial(attend_kernel, blk),
        grid=(pairs,),
        in_specs=[col(0), col(pairs), col(2 * pairs)]
        + [fixed((length, PAIR))] * 3
        + [fixed((length, 1)), fixed((1, length))],
        out_specs=[col(0)] * 4 + [pl.BlockSpec((1, 2, length), lambda p: (p, 0, 0))],
        out_shape=[jax.ShapeDtypeStruct((length, heads_wide), BF16)] * 4
        + [jax.ShapeDtypeStruct((pairs, 2, length), F32)],
        compiler_params=pltpu.CompilerParams(vmem_limit_bytes=56 << 20),
        name="attend",
    )(mixed, mixed, mixed, *tables, seg_col, seg_row)


def attend_back_kernel(blk, q_ref, k_ref, v_ref, g_ref, lse_ref, cos_ref, slo_ref, shi_ref,
                       segc_ref, segr_ref, dq_ref, dk_ref, dv_ref, dk_acc, dv_acc):
    length = q_ref.shape[0]
    q_low, k_low, v_low, g_low = q_ref[...], k_ref[...], v_ref[...], g_ref[...]
    lane = lax.broadcasted_iota(jnp.int32, (1, PAIR), 1)
    k_t = k_low.T
    zero = jnp.zeros((), BF16)
    cosine, slo, shi = cos_ref[...], slo_ref[...], shi_ref[...]
    first = lane < HEAD_DIM
    count = length // blk
    for b in reversed(range(count)):
        rows = slice(b * blk, (b + 1) * blk)
        keys = (b + 1) * blk
        mask = allowed_mask(segc_ref[:keys, :1], segr_ref[:1, rows], 0, keys, b * blk, blk)
        dq_t, dk_h, dv_h = [], [], []
        for h in range(2):
            mine = first if h == 0 else jnp.logical_not(first)
            qh = jnp.where(mine, q_low[rows], zero)
            gh = jnp.where(mine, g_low[rows], zero)
            s = jnp.where(mask, nt(k_low[:keys], qh), NEG)
            p = jnp.exp(s - lse_ref[0, h : h + 1, rows])
            dp = nt(v_low[:keys], gh)
            delta = jnp.sum(p * dp, axis=0, keepdims=True)
            ds = (p * (dp - delta)).astype(BF16)
            dq_t.append(nn(k_t[h * HEAD_DIM : (h + 1) * HEAD_DIM, :keys], ds))
            dk_h.append(nn(ds, q_low[rows]))
            dv_h.append(nn(p.astype(BF16), g_low[rows]))
        dk_new = jnp.where(first, dk_h[0], dk_h[1])
        dv_new = jnp.where(first, dv_h[0], dv_h[1])
        if b == count - 1:
            dk_acc[...] = dk_new
            dv_acc[...] = dv_new
        else:
            dk_acc[:keys] += dk_new
            dv_acc[:keys] += dv_new
        dq = jnp.concatenate(dq_t, 0).T * (HEAD_DIM**-0.5)
        dq_ref[rows, :] = rotate_pair(dq, cosine[rows], -slo[rows], -shi[rows]).astype(BF16)
    dk_ref[...] = rotate_pair(dk_acc[...], cosine, -slo, -shi).astype(BF16)
    dv_ref[...] = dv_acc[...].astype(BF16)


def attend_back(q, k, v, g, lse, tables, seg_col, seg_row, blk):
    length, heads_wide = q.shape
    pairs = heads_wide // PAIR
    col = pl.BlockSpec((length, PAIR), lambda p: (0, p))
    fixed = lambda shape: pl.BlockSpec(shape, lambda p: (0, 0))
    return pl.pallas_call(
        functools.partial(attend_back_kernel, blk),
        grid=(pairs,),
        in_specs=[col] * 4
        + [pl.BlockSpec((1, 2, length), lambda p: (p, 0, 0))]
        + [fixed((length, PAIR))] * 3
        + [fixed((length, 1)), fixed((1, length))],
        out_specs=[col] * 3,
        out_shape=[jax.ShapeDtypeStruct((length, heads_wide), BF16)] * 3,
        scratch_shapes=[pltpu.VMEM((length, PAIR), F32)] * 2,
        compiler_params=pltpu.CompilerParams(vmem_limit_bytes=56 << 20),
        name="attend_back",
    )(q, k, v, g, lse, *tables, seg_col, seg_row)


def pick(x, index, axis=0):
    return lax.dynamic_index_in_dim(x, index, axis, keepdims=False)


def shift(x, offset, count):
    return lax.ppermute(x, "shard", [(i, (i + offset) % count) for i in range(count)])


def gather_row(x, count, me):
    half = x.shape[0] // 2
    out = jnp.zeros((count,) + x.shape, x.dtype)
    out = lax.dynamic_update_slice(out, x[None], (me, 0, 0))
    fore = aft = x
    for step in range(1, count // 2):
        fore = shift(fore, 1, count)
        aft = shift(aft, -1, count)
        out = lax.dynamic_update_slice(out, fore[None], ((me - step) % count, 0, 0))
        out = lax.dynamic_update_slice(out, aft[None], ((me + step) % count, 0, 0))
    far = (me + count // 2) % count
    fore = shift(fore[:half], 1, count)
    aft = shift(aft[half:], -1, count)
    out = lax.dynamic_update_slice(out, fore[None], (far, 0, 0))
    out = lax.dynamic_update_slice(out, aft[None], (far, half, 0))
    return out.reshape(count * x.shape[0], x.shape[1])


def scatter_row(x, count, me):
    x = x.reshape(count, x.shape[0] // count, x.shape[1])
    half = x.shape[1] // 2

    def block(step):
        return pick(x, (me + step) % count)

    far = block(count // 2)
    fore = shift(far[:half], 1, count)
    aft = shift(far[half:], -1, count)
    for step in range(count // 2 - 1, 0, -1):
        ahead, behind = block(step).astype(F32), block(-step).astype(F32)
        if fore.shape[0] == half:
            ahead = jnp.concatenate([ahead[:half] + fore.astype(F32), ahead[half:]], 0)
            behind = jnp.concatenate([behind[:half], behind[half:] + aft.astype(F32)], 0)
        else:
            ahead = ahead + fore.astype(F32)
            behind = behind + aft.astype(F32)
        fore = shift(ahead.astype(BF16), 1, count)
        aft = shift(behind.astype(BF16), -1, count)
    return block(0).astype(F32) + fore.astype(F32) + aft.astype(F32)


def scatter_direct(x, count, me):
    x = x.reshape(count, x.shape[0] // count, x.shape[1])
    out = pick(x, me).astype(F32)
    for step in range(1, count):
        out = out + shift(pick(x, (me + step) % count), step, count).astype(F32)
    return out


def gather_small(x, count, me):
    out = lax.dynamic_update_slice(jnp.zeros((count,) + x.shape, x.dtype), x[None], (me, 0))
    for step in range(1, count):
        out = lax.dynamic_update_slice(out, shift(x, step, count)[None], ((me - step) % count, 0))
    return out


def swap_blocks(x, axis, count, me):
    out = jnp.zeros(x.shape, x.dtype)

    def put(out, block, place):
        start = [0] * x.ndim
        start[axis] = place
        return lax.dynamic_update_slice(out, jnp.expand_dims(block, axis), start)

    out = put(out, pick(x, me, axis), me)
    for step in range(1, count):
        block = shift(pick(x, (me + step) % count, axis), step, count)
        out = put(out, block, (me - step) % count)
    return out


def flip(x, mask, reps):
    return lax.ppermute(x, "rep", [(i, i ^ mask) for i in range(reps)])


def reduce_chips(x, rep, reps):
    lead, rows, cols = x.shape
    chips = reps // 2
    x = x.reshape(lead, chips, rows // chips, cols)
    mine = rep >> 1
    arrived = [flip(pick(x, mine ^ mask, 1), 2 * mask, reps) for mask in range(1, chips)]

    def total():
        out = pick(x, mine, 1).astype(F32)
        for term in arrived:
            out = out + term.astype(F32)
        return out.astype(BF16)

    return total


def spread(x, reps):
    own = [x] + [flip(x, 2 * mask, reps) for mask in range(1, reps // 2)]
    return own + [flip(piece, 1, reps) for piece in own]


def assemble(pieces, rep, wide):
    chips = len(pieces) // 2
    lead, rows, cols = pieces[0].shape
    tile = max(8, rows // 2)
    tiles = rows // tile
    groups, width = (1, 2 * cols * lead) if wide else (lead, 2 * cols)

    def kernel(place_ref, *refs):
        out = refs[-1]
        for i in range(chips):

            @pl.when(pl.program_id(0) == i)
            def _(i=i):
                for side, ref in ((place_ref[1], refs[i]), (1 - place_ref[1], refs[chips + i])):
                    for l in range(lead):
                        at = pl.multiple_of(side * cols + (l * 2 * cols if wide else 0), 128)
                        out[0 if wide else l, 0, :, pl.ds(at, cols)] = ref[l].astype(F32)

    def source(i):
        return pl.BlockSpec(
            (lead, tile, cols),
            lambda p, t, place: (0, jnp.where(p == i, t, jnp.where(p < i, 0, tiles - 1)), 0),
        )

    out = pl.pallas_call(
        kernel,
        grid_spec=pltpu.PrefetchScalarGridSpec(
            num_scalar_prefetch=1,
            grid=(chips, tiles),
            in_specs=[source(i) for i in range(chips)] * 2,
            out_specs=pl.BlockSpec(
                (groups, 1, tile, width), lambda p, t, place: (0, place[0] ^ p, t, 0)
            ),
        ),
        out_shape=jax.ShapeDtypeStruct((groups, chips, rows, width), F32),
        compiler_params=pltpu.CompilerParams(vmem_limit_bytes=48 << 20),
        name="assemble",
    )(jnp.stack([rep >> 1, rep & 1]), *pieces)
    return out.reshape(groups * chips * rows, width)


def lay_out(x, wide):
    reps, lead, rows, cols = x.shape
    tile = max(8, rows // 2)
    groups, width = (1, 2 * cols * lead) if wide else (lead, 2 * cols)

    def kernel(x_ref, out):
        for side in range(2):
            for l in range(lead):
                at = side * cols + (l * 2 * cols if wide else 0)
                out[0 if wide else l, 0, :, at : at + cols] = x_ref[side, l].astype(F32)

    out = pl.pallas_call(
        kernel,
        grid=(reps // 2, rows // tile),
        in_specs=[pl.BlockSpec((2, lead, tile, cols), lambda p, t: (p, 0, t, 0))],
        out_specs=pl.BlockSpec((groups, 1, tile, width), lambda p, t: (0, p, t, 0)),
        out_shape=jax.ShapeDtypeStruct((groups, reps // 2, rows, width), F32),
        compiler_params=pltpu.CompilerParams(vmem_limit_bytes=48 << 20),
        name="place",
    )(x)
    return out.reshape(groups * (reps // 2) * rows, width)


def hold(*xs):
    return lax.optimization_barrier(xs)


def local(
    tokens,
    segments,
    positions,
    norm_gain,
    norm_shift,
    inproj_weight,
    inproj_bias,
    outproj_weight,
    outproj_bias,
    expand_weight,
    expand_bias,
    shrink_weight,
    shrink_bias,
    out_grad,
):
    span, width = tokens.shape[1:]
    count = lax.axis_size("shard")
    reps = lax.axis_size("rep")
    bits = reps.bit_length() - 1
    me = lax.axis_index("shard")
    rep = lax.axis_index("rep")
    core = rep & 1
    length = span * count
    part = width // count
    inner = expand_weight.shape[0]
    sub = part // reps

    kind_of = np.zeros((count, 3), np.int32)
    forward = [[(s, (3 * s + j) % count) for s in range(count)] for j in range(3)]
    for s in range(count):
        for j in range(3):
            kind_of[(3 * s + j) % count, j] = (3 * s + j) // count
    round_of = np.argsort(kind_of, 1).astype(np.int32)

    packed = jnp.concatenate([norm_gain, norm_shift, outproj_bias, shrink_bias, inproj_bias])
    packed = gather_small(packed, count, me)
    gain, shift_all, outbias, shrbias = (
        packed[:, i * part : (i + 1) * part].reshape(width).astype(F32) for i in range(4)
    )
    inbias = packed[:, 4 * part :].reshape(3, count, part)
    inbias = pick(inbias, me, 1).reshape(3 * part).astype(F32)

    slices = lax.dynamic_slice_in_dim(inproj_weight.reshape(3, part, width), rep * sub, sub, 1)
    arrived = jnp.stack([lax.ppermute(slices[j], "shard", forward[j]) for j in range(3)])
    my_rounds = pick(jnp.asarray(round_of), me)
    arrived = jnp.stack([pick(arrived, my_rounds[k]) for k in range(3)])
    in_w = lax.all_gather(arrived, "rep", axis=1, tiled=True).reshape(3 * part, width)
    down = jnp.concatenate(
        [
            lax.dynamic_slice_in_dim(shrink_weight, rep * sub, sub, 0).reshape(sub, count, inner),
            lax.dynamic_slice_in_dim(outproj_weight, rep * sub, sub, 0).reshape(sub, count, part),
        ],
        2,
    )
    down = swap_blocks(jnp.transpose(down, (1, 0, 2)), 0, count, me)
    shrink_w = lax.all_gather(down[:, :, :inner], "rep", axis=1, tiled=True).reshape(width, inner)
    out_w = lax.all_gather(down[:, :, inner:], "rep", axis=1, tiled=True).reshape(width, part)

    residual = tokens.reshape(span, width).astype(F32)
    row_mean = jnp.mean(residual, -1, keepdims=True)
    centered = residual - row_mean
    row_var = jnp.mean(centered * centered, -1, keepdims=True)
    inv_std = lax.rsqrt(row_var + 1e-05)
    xhat = centered * inv_std
    normed_own = (xhat * gain + shift_all).astype(BF16)
    normed = gather_row(normed_own, count, me)

    grad_own = out_grad.reshape(span, width)
    grads = gather_row(grad_own, count, me)

    seg = segments.reshape(length)
    starts = jnp.sum((seg[None, :] < seg[:, None]).astype(jnp.int32), 1)
    place = (jnp.arange(length, dtype=jnp.int32) - starts).astype(F32)
    lane = jnp.arange(PAIR) % HEAD_DIM
    inverse_freq = 10000.0 ** (-(lane % (ROT // 2)).astype(F32) * 2.0 / ROT)
    angle = place[:, None] * inverse_freq[None, :]
    sine = jnp.sin(angle)
    tables = (
        jnp.where(lane < ROT, jnp.cos(angle), 1.0),
        jnp.where(lane < ROT // 2, -sine, 0.0),
        jnp.where((lane >= ROT // 2) & (lane < ROT), sine, 0.0),
    )
    seg_col, seg_row = seg[:, None], seg[None, :]
    blk = min(256, length)
    back = [[(b, a) for a, b in pairs] for pairs in forward]

    def col_half(x, which):
        wide = x.shape[1] // 2
        return lax.dynamic_slice_in_dim(x, which * wide, wide, 1)

    def low_term(outputs, inputs, extra=None):
        out = tn(outputs, inputs)
        return (out if extra is None else out + extra.astype(F32)).astype(BF16)

    normed_mine, normed_other = col_half(normed, core), col_half(normed, 1 - core)
    expanded = nt(normed, expand_weight) + expand_bias.astype(F32)
    hidden, slope = gelu_parts(expanded)
    hidden, slope = hidden.astype(BF16), slope.astype(BF16)
    hidden_mine, hidden_other = col_half(hidden, core), col_half(hidden, 1 - core)
    normed_1, hidden = hold(normed, hidden)
    mixed = nt(normed_1, in_w) + inbias
    attended, q_low, k_low, v_low, lse = attend(mixed, tables, seg_col, seg_row, blk)
    hidden_1, attended = hold(hidden, attended)
    branches = (nt(hidden_1, shrink_w) + nt(attended, out_w)).astype(BF16)
    branches_sum = scatter_direct(branches, count, me)

    grads, branches = hold(grads, branches)
    blocks = inner // part
    shr_send = low_term(grads, hidden_other)
    shr_arrived = flip(shr_send, 1, reps)
    grads_1, shr_send = hold(grads, shr_send)
    d_up = (nn(grads_1, shrink_w) * slope.astype(F32)).astype(BF16)
    grads_2, d_up = hold(grads_1, d_up)
    shr_sum = low_term(grads_2, hidden_mine, shr_arrived)
    shr_total = reduce_chips(shr_sum.reshape(count, part, inner // 2), rep, reps)
    d_up, shr_sum = hold(d_up, shr_sum)
    exp_send = low_term(d_up, normed_other)
    exp_arrived = flip(exp_send, 1, reps)
    grads_3, exp_send = hold(grads_2, exp_send)
    d_att = nn(grads_3, out_w).astype(BF16)
    d_up_1, d_att = hold(d_up, d_att)
    exp_sum = low_term(d_up_1, normed_mine, exp_arrived)
    exp_total = reduce_chips(exp_sum.reshape(blocks, part, width // 2), rep, reps)

    grads_4, exp_sum = hold(grads_3, exp_sum)
    g_out_1 = tn(grads_4, attended).astype(BF16)
    g_out = lax.psum_scatter(
        g_out_1.reshape(count, part, part), "rep", scatter_dimension=1, tiled=True
    )
    d_att, g_out_1 = hold(d_att, g_out_1)
    d_q, d_k, d_v = attend_back(q_low, k_low, v_low, d_att, lse, tables, seg_col, seg_row, blk)
    d_mixed = jnp.concatenate([d_q, d_k, d_v], 1)
    in_send = low_term(d_mixed, normed_other)
    in_arrived = flip(in_send, 1, reps)
    g_shr = shr_total()
    d_mixed_1, in_send, g_shr = hold(d_mixed, in_send, g_shr)
    g_shr = swap_blocks(g_shr, 0, count, me)
    g_shr = lax.all_gather(g_shr, "rep", axis=0)
    g_out = jnp.transpose(swap_blocks(g_out, 0, count, me), (1, 0, 2)).reshape(sub, width)
    in_sum = low_term(d_mixed_1, normed_mine, in_arrived)
    in_total = reduce_chips(in_sum.reshape(3, part, width // 2), rep, reps)
    d_mixed_2, d_up_2, in_sum = hold(d_mixed_1, d_up_1, in_sum)
    b_out = jnp.sum(lax.dynamic_slice_in_dim(grads_4, me * part, part, 1), 0, dtype=F32)
    b_exp = jnp.sum(d_up_2, 0, dtype=F32)
    b_in = jnp.sum(d_mixed_2, 0, dtype=F32)
    g_exp = exp_total()
    exp_pieces = spread(g_exp, reps)
    d_mixed_2, b_in, g_exp = hold(d_mixed_2, b_in, g_exp)
    d_normed = nn(d_up_2, expand_weight) + nn(d_mixed_2, in_w)
    both = jnp.stack([jnp.sum(d_normed * normed.astype(F32), 0), jnp.sum(d_normed, 0)])
    d_normed = d_normed.astype(BF16)
    d_normed = scatter_row(d_normed, count, me)
    kinds = pick(jnp.asarray(kind_of), me)
    g_in = in_total()
    both, g_in = hold(both, g_in)
    g_in = jnp.stack([lax.ppermute(pick(g_in, kinds[j]), "shard", back[j]) for j in range(3)])
    in_pieces = spread(g_in, reps)

    both = jnp.sum(swap_blocks(both.reshape(2, count, part), 1, count, me), 1)
    sums = jnp.concatenate([both[0], both[1], b_out, b_exp, b_in])

    g_out = lax.all_gather(g_out, "rep", axis=0, tiled=True).astype(F32)
    g_shr = lay_out(g_shr, True)
    g_exp = assemble(exp_pieces, rep, False)
    g_in = assemble(in_pieces, rep, False)
    block_output = (residual + (branches_sum + (outbias + shrbias))).astype(BF16)

    d_hat = d_normed * gain
    token_grad = grad_own.astype(F32) + inv_std * (
        d_hat
        - jnp.mean(d_hat, -1, keepdims=True)
        - xhat * jnp.mean(d_hat * xhat, -1, keepdims=True)
    )

    for bit in range(bits):
        sums = sums + flip(sums, 1 << bit, reps)
    b_norm, b_shift, b_out = sums[:part], sums[part : 2 * part], sums[2 * part : 3 * part]
    b_gain = (b_norm - norm_shift.astype(F32) * b_shift) / norm_gain.astype(F32)
    b_exp, b_in = sums[3 * part : 3 * part + inner], sums[3 * part + inner :].reshape(3, part)
    b_in = jnp.concatenate([lax.ppermute(pick(b_in, kinds[j]), "shard", back[j]) for j in range(3)])

    return (
        block_output[None],
        token_grad[None],
        b_gain,
        b_shift,
        g_in,
        b_in,
        g_out,
        b_out,
        g_exp,
        b_exp,
        g_shr,
        b_out,
    )


def solution(mesh):
    in_specs = (
        P("rep", "shard", None),
        P("rep", None),
        P("rep", "shard"),
        P("shard"),
        P("shard"),
        P("shard", None),
        P("shard"),
        P("shard", None),
        P("shard"),
        P("shard", None),
        P("shard"),
        P("shard", None),
        P("shard"),
        P("rep", "shard", None),
    )
    out_specs = (
        P("rep", "shard", None),
        P("rep", "shard", None),
        P("shard"),
        P("shard"),
        P("shard", None),
        P("shard"),
        P("shard", None),
        P("shard"),
        P("shard", None),
        P("shard"),
        P("shard", None),
        P("shard"),
    )

    return jax.shard_map(local, mesh=mesh, in_specs=in_specs, out_specs=out_specs, check_vma=False)
```

```python
import functools
import math

import jax
import jax.numpy as jnp
import numpy as np
from jax import lax
from jax.experimental import pallas as pl
from jax.experimental.pallas import tpu as pltpu
from jax.sharding import PartitionSpec as P


HEAD_DIM = 64
ROT = 32
PAIR = 2 * HEAD_DIM
NEG = -1e30
F32 = jnp.float32
BF16 = jnp.bfloat16


def nt(a, b):
    return lax.dot_general(a, b, (((1,), (1,)), ((), ())), preferred_element_type=F32)


def nn(a, b):
    return lax.dot_general(a, b, (((1,), (0,)), ((), ())), preferred_element_type=F32)


def tn(a, b):
    return lax.dot_general(a, b, (((0,), (0,)), ((), ())), preferred_element_type=F32)


def gelu_parts(values):
    c = math.sqrt(2.0 / math.pi)
    square = values * values
    t = jnp.tanh(c * (values + 0.044715 * square * values))
    half = 0.5 * (1.0 + t)
    slope = half + 0.5 * values * (1.0 - t * t) * (c * (1.0 + 3.0 * 0.044715 * square))
    return values * half, slope


def rotate_pair(x, cosine, sine_low, sine_high):
    quarter = ROT // 2
    up = pltpu.roll(x, PAIR - quarter, 1)
    down = pltpu.roll(x, quarter, 1)
    return x * cosine + up * sine_low + down * sine_high


def allowed_mask(seg_col, seg_row, first_key, keys, first_query, queries):
    same = seg_col == seg_row
    kpos = first_key + lax.broadcasted_iota(jnp.int32, (keys, queries), 0)
    qpos = first_query + lax.broadcasted_iota(jnp.int32, (keys, queries), 1)
    return same & (kpos <= qpos)


def attend_kernel(blk, q_ref, k_ref, v_ref, cos_ref, slo_ref, shi_ref, segc_ref, segr_ref,
                  o_ref, q_out, k_out, v_out, lse_ref):
    length = q_ref.shape[0]
    cosine, slo, shi = cos_ref[...], slo_ref[...], shi_ref[...]
    q_low = (rotate_pair(q_ref[...], cosine, slo, shi).astype(BF16)) * jnp.asarray(HEAD_DIM**-0.5, BF16)
    k_low = rotate_pair(k_ref[...], cosine, slo, shi).astype(BF16)
    v_low = v_ref[...].astype(BF16)
    q_out[...] = q_low
    k_out[...] = k_low
    v_out[...] = v_low
    lane = lax.broadcasted_iota(jnp.int32, (1, PAIR), 1)
    v_t = v_low.T
    for b in range(length // blk):
        rows = slice(b * blk, (b + 1) * blk)
        keys = (b + 1) * blk
        mask = allowed_mask(segc_ref[:keys, :1], segr_ref[:1, rows], 0, keys, b * blk, blk)
        outs = []
        for h in range(2):
            mine = (lane < HEAD_DIM) if h == 0 else (lane >= HEAD_DIM)
            qh = jnp.where(mine, q_low[rows], jnp.zeros((), BF16))
            s = jnp.where(mask, nt(k_low[:keys], qh), NEG)
            top = jnp.max(s, axis=0, keepdims=True)
            e = jnp.exp(s - top)
            total = jnp.sum(e, axis=0, keepdims=True)
            p = (e * (1.0 / total)).astype(BF16)
            lse_ref[0, h : h + 1, rows] = top + jnp.log(total)
            outs.append(nn(v_t[h * HEAD_DIM : (h + 1) * HEAD_DIM, :keys], p))
        o_ref[rows, :] = jnp.concatenate(outs, 0).T.astype(BF16)


def attend(mixed, tables, seg_col, seg_row, blk):
    length, wide = mixed.shape
    heads_wide = wide // 3
    pairs = heads_wide // PAIR
    col = lambda off: pl.BlockSpec((length, PAIR), lambda p: (0, off + p))
    fixed = lambda shape: pl.BlockSpec(shape, lambda p: (0, 0))
    return pl.pallas_call(
        functools.partial(attend_kernel, blk),
        grid=(pairs,),
        in_specs=[col(0), col(pairs), col(2 * pairs)]
        + [fixed((length, PAIR))] * 3
        + [fixed((length, 1)), fixed((1, length))],
        out_specs=[col(0)] * 4 + [pl.BlockSpec((1, 2, length), lambda p: (p, 0, 0))],
        out_shape=[jax.ShapeDtypeStruct((length, heads_wide), BF16)] * 4
        + [jax.ShapeDtypeStruct((pairs, 2, length), F32)],
        compiler_params=pltpu.CompilerParams(vmem_limit_bytes=56 << 20),
        name="attend",
    )(mixed, mixed, mixed, *tables, seg_col, seg_row)


def attend_back_kernel(blk, q_ref, k_ref, v_ref, g_ref, lse_ref, cos_ref, slo_ref, shi_ref,
                       segc_ref, segr_ref, dq_ref, dk_ref, dv_ref, dk_acc, dv_acc):
    length = q_ref.shape[0]
    q_low, k_low, v_low, g_low = q_ref[...], k_ref[...], v_ref[...], g_ref[...]
    lane = lax.broadcasted_iota(jnp.int32, (1, PAIR), 1)
    k_t = k_low.T
    zero = jnp.zeros((), BF16)
    cosine, slo, shi = cos_ref[...], slo_ref[...], shi_ref[...]
    first = lane < HEAD_DIM
    count = length // blk
    for b in reversed(range(count)):
        rows = slice(b * blk, (b + 1) * blk)
        keys = (b + 1) * blk
        mask = allowed_mask(segc_ref[:keys, :1], segr_ref[:1, rows], 0, keys, b * blk, blk)
        dq_t, dk_h, dv_h = [], [], []
        for h in range(2):
            mine = first if h == 0 else jnp.logical_not(first)
            qh = jnp.where(mine, q_low[rows], zero)
            gh = jnp.where(mine, g_low[rows], zero)
            s = jnp.where(mask, nt(k_low[:keys], qh), NEG)
            p = jnp.exp(s - lse_ref[0, h : h + 1, rows])
            dp = nt(v_low[:keys], gh)
            delta = jnp.sum(p * dp, axis=0, keepdims=True)
            ds = (p * (dp - delta)).astype(BF16)
            dq_t.append(nn(k_t[h * HEAD_DIM : (h + 1) * HEAD_DIM, :keys], ds))
            dk_h.append(nn(ds, q_low[rows]))
            dv_h.append(nn(p.astype(BF16), g_low[rows]))
        dk_new = jnp.where(first, dk_h[0], dk_h[1])
        dv_new = jnp.where(first, dv_h[0], dv_h[1])
        if b == count - 1:
            dk_acc[...] = dk_new
            dv_acc[...] = dv_new
        else:
            dk_acc[:keys] += dk_new
            dv_acc[:keys] += dv_new
        dq = jnp.concatenate(dq_t, 0).T * (HEAD_DIM**-0.5)
        dq_ref[rows, :] = rotate_pair(dq, cosine[rows], -slo[rows], -shi[rows]).astype(BF16)
    dk_ref[...] = rotate_pair(dk_acc[...], cosine, -slo, -shi).astype(BF16)
    dv_ref[...] = dv_acc[...].astype(BF16)


def attend_back(q, k, v, g, lse, tables, seg_col, seg_row, blk):
    length, heads_wide = q.shape
    pairs = heads_wide // PAIR
    col = pl.BlockSpec((length, PAIR), lambda p: (0, p))
    fixed = lambda shape: pl.BlockSpec(shape, lambda p: (0, 0))
    return pl.pallas_call(
        functools.partial(attend_back_kernel, blk),
        grid=(pairs,),
        in_specs=[col] * 4
        + [pl.BlockSpec((1, 2, length), lambda p: (p, 0, 0))]
        + [fixed((length, PAIR))] * 3
        + [fixed((length, 1)), fixed((1, length))],
        out_specs=[col] * 3,
        out_shape=[jax.ShapeDtypeStruct((length, heads_wide), BF16)] * 3,
        scratch_shapes=[pltpu.VMEM((length, PAIR), F32)] * 2,
        compiler_params=pltpu.CompilerParams(vmem_limit_bytes=56 << 20),
        name="attend_back",
    )(q, k, v, g, lse, *tables, seg_col, seg_row)


def pick(x, index, axis=0):
    return lax.dynamic_index_in_dim(x, index, axis, keepdims=False)


def shift(x, offset, count):
    return lax.ppermute(x, "shard", [(i, (i + offset) % count) for i in range(count)])


def gather_row(x, count, me):
    half = x.shape[0] // 2
    out = jnp.zeros((count,) + x.shape, x.dtype)
    out = lax.dynamic_update_slice(out, x[None], (me, 0, 0))
    fore = aft = x
    for step in range(1, count // 2):
        fore = shift(fore, 1, count)
        aft = shift(aft, -1, count)
        out = lax.dynamic_update_slice(out, fore[None], ((me - step) % count, 0, 0))
        out = lax.dynamic_update_slice(out, aft[None], ((me + step) % count, 0, 0))
    far = (me + count // 2) % count
    fore = shift(fore[:half], 1, count)
    aft = shift(aft[half:], -1, count)
    out = lax.dynamic_update_slice(out, fore[None], (far, 0, 0))
    out = lax.dynamic_update_slice(out, aft[None], (far, half, 0))
    return out.reshape(count * x.shape[0], x.shape[1])


def scatter_row(x, count, me):
    x = x.reshape(count, x.shape[0] // count, x.shape[1])
    half = x.shape[1] // 2

    def block(step):
        return pick(x, (me + step) % count)

    far = block(count // 2)
    fore = shift(far[:half], 1, count)
    aft = shift(far[half:], -1, count)
    for step in range(count // 2 - 1, 0, -1):
        ahead, behind = block(step).astype(F32), block(-step).astype(F32)
        if fore.shape[0] == half:
            ahead = jnp.concatenate([ahead[:half] + fore.astype(F32), ahead[half:]], 0)
            behind = jnp.concatenate([behind[:half], behind[half:] + aft.astype(F32)], 0)
        else:
            ahead = ahead + fore.astype(F32)
            behind = behind + aft.astype(F32)
        fore = shift(ahead.astype(BF16), 1, count)
        aft = shift(behind.astype(BF16), -1, count)
    return block(0).astype(F32) + fore.astype(F32) + aft.astype(F32)


def scatter_direct(x, count, me):
    x = x.reshape(count, x.shape[0] // count, x.shape[1])
    out = pick(x, me).astype(F32)
    for step in range(1, count):
        out = out + shift(pick(x, (me + step) % count), step, count).astype(F32)
    return out


def gather_small(x, count, me):
    out = lax.dynamic_update_slice(jnp.zeros((count,) + x.shape, x.dtype), x[None], (me, 0))
    for step in range(1, count):
        out = lax.dynamic_update_slice(out, shift(x, step, count)[None], ((me - step) % count, 0))
    return out


def swap_blocks(x, axis, count, me):
    out = jnp.zeros(x.shape, x.dtype)

    def put(out, block, place):
        start = [0] * x.ndim
        start[axis] = place
        return lax.dynamic_update_slice(out, jnp.expand_dims(block, axis), start)

    out = put(out, pick(x, me, axis), me)
    for step in range(1, count):
        block = shift(pick(x, (me + step) % count, axis), step, count)
        out = put(out, block, (me - step) % count)
    return out


def flip(x, mask, reps):
    return lax.ppermute(x, "rep", [(i, i ^ mask) for i in range(reps)])


def reduce_chips(x, rep, reps):
    lead, rows, cols = x.shape
    chips = reps // 2
    x = x.reshape(lead, chips, rows // chips, cols)
    mine = rep >> 1
    arrived = [flip(pick(x, mine ^ mask, 1), 2 * mask, reps) for mask in range(1, chips)]

    def total():
        out = pick(x, mine, 1).astype(F32)
        for term in arrived:
            out = out + term.astype(F32)
        return out.astype(BF16)

    return total


def spread(x, reps):
    own = [x] + [flip(x, 2 * mask, reps) for mask in range(1, reps // 2)]
    return own + [flip(piece, 1, reps) for piece in own]


def assemble(pieces, rep, wide):
    chips = len(pieces) // 2
    lead, rows, cols = pieces[0].shape
    tile = max(8, rows // 2)
    tiles = rows // tile
    groups, width = (1, 2 * cols * lead) if wide else (lead, 2 * cols)

    def kernel(place_ref, *refs):
        out = refs[-1]
        for i in range(chips):

            @pl.when(pl.program_id(0) == i)
            def _(i=i):
                for side, ref in ((place_ref[1], refs[i]), (1 - place_ref[1], refs[chips + i])):
                    for l in range(lead):
                        at = pl.multiple_of(side * cols + (l * 2 * cols if wide else 0), 128)
                        out[0 if wide else l, 0, :, pl.ds(at, cols)] = ref[l].astype(F32)

    def source(i):
        return pl.BlockSpec(
            (lead, tile, cols),
            lambda p, t, place: (0, jnp.where(p == i, t, jnp.where(p < i, 0, tiles - 1)), 0),
        )

    out = pl.pallas_call(
        kernel,
        grid_spec=pltpu.PrefetchScalarGridSpec(
            num_scalar_prefetch=1,
            grid=(chips, tiles),
            in_specs=[source(i) for i in range(chips)] * 2,
            out_specs=pl.BlockSpec(
                (groups, 1, tile, width), lambda p, t, place: (0, place[0] ^ p, t, 0)
            ),
        ),
        out_shape=jax.ShapeDtypeStruct((groups, chips, rows, width), F32),
        compiler_params=pltpu.CompilerParams(vmem_limit_bytes=48 << 20),
        name="assemble",
    )(jnp.stack([rep >> 1, rep & 1]), *pieces)
    return out.reshape(groups * chips * rows, width)


def lay_out(x, wide):
    reps, lead, rows, cols = x.shape
    tile = max(8, rows // 2)
    groups, width = (1, 2 * cols * lead) if wide else (lead, 2 * cols)

    def kernel(x_ref, out):
        for side in range(2):
            for l in range(lead):
                at = side * cols + (l * 2 * cols if wide else 0)
                out[0 if wide else l, 0, :, at : at + cols] = x_ref[side, l].astype(F32)

    out = pl.pallas_call(
        kernel,
        grid=(reps // 2, rows // tile),
        in_specs=[pl.BlockSpec((2, lead, tile, cols), lambda p, t: (p, 0, t, 0))],
        out_specs=pl.BlockSpec((groups, 1, tile, width), lambda p, t: (0, p, t, 0)),
        out_shape=jax.ShapeDtypeStruct((groups, reps // 2, rows, width), F32),
        compiler_params=pltpu.CompilerParams(vmem_limit_bytes=48 << 20),
        name="place",
    )(x)
    return out.reshape(groups * (reps // 2) * rows, width)


def hold(*xs):
    return lax.optimization_barrier(xs)


def local(
    tokens,
    segments,
    positions,
    norm_gain,
    norm_shift,
    inproj_weight,
    inproj_bias,
    outproj_weight,
    outproj_bias,
    expand_weight,
    expand_bias,
    shrink_weight,
    shrink_bias,
    out_grad,
):
    span, width = tokens.shape[1:]
    count = lax.axis_size("shard")
    reps = lax.axis_size("rep")
    bits = reps.bit_length() - 1
    me = lax.axis_index("shard")
    rep = lax.axis_index("rep")
    core = rep & 1
    length = span * count
    part = width // count
    inner = expand_weight.shape[0]
    sub = part // reps

    kind_of = np.zeros((count, 3), np.int32)
    forward = [[(s, (3 * s + j) % count) for s in range(count)] for j in range(3)]
    for s in range(count):
        for j in range(3):
            kind_of[(3 * s + j) % count, j] = (3 * s + j) // count
    round_of = np.argsort(kind_of, 1).astype(np.int32)

    packed = jnp.concatenate([norm_gain, norm_shift, outproj_bias, shrink_bias, inproj_bias])
    packed = gather_small(packed, count, me)
    gain, shift_all, outbias, shrbias = (
        packed[:, i * part : (i + 1) * part].reshape(width).astype(F32) for i in range(4)
    )
    inbias = packed[:, 4 * part :].reshape(3, count, part)
    inbias = pick(inbias, me, 1).reshape(3 * part).astype(F32)

    slices = lax.dynamic_slice_in_dim(inproj_weight.reshape(3, part, width), rep * sub, sub, 1)
    arrived = jnp.stack([lax.ppermute(slices[j], "shard", forward[j]) for j in range(3)])
    my_rounds = pick(jnp.asarray(round_of), me)
    arrived = jnp.stack([pick(arrived, my_rounds[k]) for k in range(3)])
    in_w = lax.all_gather(arrived, "rep", axis=1, tiled=True).reshape(3 * part, width)
    down = jnp.concatenate(
        [
            lax.dynamic_slice_in_dim(shrink_weight, rep * sub, sub, 0).reshape(sub, count, inner),
            lax.dynamic_slice_in_dim(outproj_weight, rep * sub, sub, 0).reshape(sub, count, part),
        ],
        2,
    )
    down = swap_blocks(jnp.transpose(down, (1, 0, 2)), 0, count, me)
    shrink_w = lax.all_gather(down[:, :, :inner], "rep", axis=1, tiled=True).reshape(width, inner)
    out_w = lax.all_gather(down[:, :, inner:], "rep", axis=1, tiled=True).reshape(width, part)

    residual = tokens.reshape(span, width).astype(F32)
    row_mean = jnp.mean(residual, -1, keepdims=True)
    centered = residual - row_mean
    row_var = jnp.mean(centered * centered, -1, keepdims=True)
    inv_std = lax.rsqrt(row_var + 1e-05)
    xhat = centered * inv_std
    normed_own = (xhat * gain + shift_all).astype(BF16)
    normed = gather_row(normed_own, count, me)

    grad_own = out_grad.reshape(span, width)
    grads = gather_row(grad_own, count, me)

    seg = segments.reshape(length)
    starts = jnp.sum((seg[None, :] < seg[:, None]).astype(jnp.int32), 1)
    place = (jnp.arange(length, dtype=jnp.int32) - starts).astype(F32)
    lane = jnp.arange(PAIR) % HEAD_DIM
    inverse_freq = 10000.0 ** (-(lane % (ROT // 2)).astype(F32) * 2.0 / ROT)
    angle = place[:, None] * inverse_freq[None, :]
    sine = jnp.sin(angle)
    tables = (
        jnp.where(lane < ROT, jnp.cos(angle), 1.0),
        jnp.where(lane < ROT // 2, -sine, 0.0),
        jnp.where((lane >= ROT // 2) & (lane < ROT), sine, 0.0),
    )
    seg_col, seg_row = seg[:, None], seg[None, :]
    blk = min(256, length)
    back = [[(b, a) for a, b in pairs] for pairs in forward]

    def col_half(x, which):
        wide = x.shape[1] // 2
        return lax.dynamic_slice_in_dim(x, which * wide, wide, 1)

    def low_term(outputs, inputs, extra=None):
        out = tn(outputs, inputs)
        return (out if extra is None else out + extra.astype(F32)).astype(BF16)

    normed_mine, normed_other = col_half(normed, core), col_half(normed, 1 - core)
    expanded = nt(normed, expand_weight) + expand_bias.astype(F32)
    hidden, slope = gelu_parts(expanded)
    hidden, slope = hidden.astype(BF16), slope.astype(BF16)
    hidden_mine, hidden_other = col_half(hidden, core), col_half(hidden, 1 - core)
    normed_1, hidden = hold(normed, hidden)
    mixed = nt(normed_1, in_w) + inbias
    attended, q_low, k_low, v_low, lse = attend(mixed, tables, seg_col, seg_row, blk)
    hidden_1, attended = hold(hidden, attended)
    branches = (nt(hidden_1, shrink_w) + nt(attended, out_w)).astype(BF16)
    branches_sum = scatter_direct(branches, count, me)

    grads, branches = hold(grads, branches)
    blocks = inner // part
    shr_send = low_term(grads, hidden_other)
    shr_arrived = flip(shr_send, 1, reps)
    grads_1, shr_send = hold(grads, shr_send)
    d_up = (nn(grads_1, shrink_w) * slope.astype(F32)).astype(BF16)
    grads_2, d_up = hold(grads_1, d_up)
    shr_sum = low_term(grads_2, hidden_mine, shr_arrived)
    shr_total = reduce_chips(shr_sum.reshape(count, part, inner // 2), rep, reps)
    d_up, shr_sum = hold(d_up, shr_sum)
    exp_send = low_term(d_up, normed_other)
    exp_arrived = flip(exp_send, 1, reps)
    grads_3, exp_send = hold(grads_2, exp_send)
    d_att = nn(grads_3, out_w).astype(BF16)
    d_up_1, d_att = hold(d_up, d_att)
    exp_sum = low_term(d_up_1, normed_mine, exp_arrived)
    exp_total = reduce_chips(exp_sum.reshape(blocks, part, width // 2), rep, reps)

    grads_4, exp_sum = hold(grads_3, exp_sum)
    g_out = tn(grads_4, attended).astype(BF16)
    g_out_1 = lax.psum_scatter(
        g_out.reshape(count, part, part), "rep", scatter_dimension=1, tiled=True
    )
    d_up_2, g_out = hold(d_up_1, g_out)
    d_normed = nn(d_up_2, expand_weight)
    g_shr = shr_total()
    d_att, d_normed, g_shr = hold(d_att, d_normed, g_shr)
    g_shr = swap_blocks(g_shr, 0, count, me)
    g_shr = lax.all_gather(g_shr, "rep", axis=0)
    d_q, d_k, d_v = attend_back(q_low, k_low, v_low, d_att, lse, tables, seg_col, seg_row, blk)
    d_mixed = jnp.concatenate([d_q, d_k, d_v], 1)
    in_send = low_term(d_mixed, normed_other)
    in_arrived = flip(in_send, 1, reps)
    d_mixed_1, in_send = hold(d_mixed, in_send)
    b_out = jnp.sum(lax.dynamic_slice_in_dim(grads_3, me * part, part, 1), 0, dtype=F32)
    b_exp = jnp.sum(d_up_2, 0, dtype=F32)
    b_in = jnp.sum(d_mixed_1, 0, dtype=F32)
    d_mixed_1, b_in = hold(d_mixed_1, b_in)
    in_sum = low_term(d_mixed_1, normed_mine, in_arrived)
    in_total = reduce_chips(in_sum.reshape(3, part, width // 2), rep, reps)
    d_mixed_2, in_sum = hold(d_mixed_1, in_sum)
    g_exp = exp_total()
    exp_pieces = spread(g_exp, reps)
    d_mixed_2, g_exp, g_out_1 = hold(d_mixed_2, g_exp, g_out_1)
    d_normed = d_normed + nn(d_mixed_2, in_w)
    both = jnp.stack([jnp.sum(d_normed * normed.astype(F32), 0), jnp.sum(d_normed, 0)])
    d_normed = d_normed.astype(BF16)
    d_normed = scatter_row(d_normed, count, me)
    kinds = pick(jnp.asarray(kind_of), me)
    g_in = in_total()
    g_in = jnp.stack([lax.ppermute(pick(g_in, kinds[j]), "shard", back[j]) for j in range(3)])
    in_pieces = spread(g_in, reps)

    both = jnp.sum(swap_blocks(both.reshape(2, count, part), 1, count, me), 1)
    sums = jnp.concatenate([both[0], both[1], b_out, b_exp, b_in])

    g_out = jnp.transpose(swap_blocks(g_out_1, 0, count, me), (1, 0, 2)).reshape(sub, width)
    g_out = lax.all_gather(g_out, "rep", axis=0, tiled=True).astype(F32)
    g_shr = lay_out(g_shr, True)
    g_exp = assemble(exp_pieces, rep, False)
    g_in = assemble(in_pieces, rep, False)
    block_output = (residual + (branches_sum + (outbias + shrbias))).astype(BF16)

    d_hat = d_normed * gain
    token_grad = grad_own.astype(F32) + inv_std * (
        d_hat
        - jnp.mean(d_hat, -1, keepdims=True)
        - xhat * jnp.mean(d_hat * xhat, -1, keepdims=True)
    )

    for bit in range(bits):
        sums = sums + flip(sums, 1 << bit, reps)
    b_norm, b_shift, b_out = sums[:part], sums[part : 2 * part], sums[2 * part : 3 * part]
    b_gain = (b_norm - norm_shift.astype(F32) * b_shift) / norm_gain.astype(F32)
    b_exp, b_in = sums[3 * part : 3 * part + inner], sums[3 * part + inner :].reshape(3, part)
    b_in = jnp.concatenate([lax.ppermute(pick(b_in, kinds[j]), "shard", back[j]) for j in range(3)])

    return (
        block_output[None],
        token_grad[None],
        b_gain,
        b_shift,
        g_in,
        b_in,
        g_out,
        b_out,
        g_exp,
        b_exp,
        g_shr,
        b_out,
    )


def solution(mesh):
    in_specs = (
        P("rep", "shard", None),
        P("rep", None),
        P("rep", "shard"),
        P("shard"),
        P("shard"),
        P("shard", None),
        P("shard"),
        P("shard", None),
        P("shard"),
        P("shard", None),
        P("shard"),
        P("shard", None),
        P("shard"),
        P("rep", "shard", None),
    )
    out_specs = (
        P("rep", "shard", None),
        P("rep", "shard", None),
        P("shard"),
        P("shard"),
        P("shard", None),
        P("shard"),
        P("shard", None),
        P("shard"),
        P("shard", None),
        P("shard"),
        P("shard", None),
        P("shard"),
    )

    return jax.shard_map(local, mesh=mesh, in_specs=in_specs, out_specs=out_specs, check_vma=False)
```

```python
import functools
import math

import jax
import jax.numpy as jnp
import numpy as np
from jax import lax
from jax.experimental import pallas as pl
from jax.experimental.pallas import tpu as pltpu
from jax.sharding import PartitionSpec as P


HEAD_DIM = 64
ROT = 32
PAIR = 2 * HEAD_DIM
NEG = -1e30
F32 = jnp.float32
BF16 = jnp.bfloat16


def nt(a, b):
    return lax.dot_general(a, b, (((1,), (1,)), ((), ())), preferred_element_type=F32)


def nn(a, b):
    return lax.dot_general(a, b, (((1,), (0,)), ((), ())), preferred_element_type=F32)


def tn(a, b):
    return lax.dot_general(a, b, (((0,), (0,)), ((), ())), preferred_element_type=F32)


def gelu_parts(values):
    c = math.sqrt(2.0 / math.pi)
    square = values * values
    t = jnp.tanh(c * (values + 0.044715 * square * values))
    half = 0.5 * (1.0 + t)
    slope = half + 0.5 * values * (1.0 - t * t) * (c * (1.0 + 3.0 * 0.044715 * square))
    return values * half, slope


def rotate_pair(x, cosine, sine_low, sine_high):
    quarter = ROT // 2
    up = pltpu.roll(x, PAIR - quarter, 1)
    down = pltpu.roll(x, quarter, 1)
    return x * cosine + up * sine_low + down * sine_high


def allowed_mask(seg_col, seg_row, first_key, keys, first_query, queries):
    same = seg_col == seg_row
    kpos = first_key + lax.broadcasted_iota(jnp.int32, (keys, queries), 0)
    qpos = first_query + lax.broadcasted_iota(jnp.int32, (keys, queries), 1)
    return same & (kpos <= qpos)


def attend_kernel(blk, q_ref, k_ref, v_ref, cos_ref, slo_ref, shi_ref, segc_ref, segr_ref,
                  o_ref, q_out, k_out, v_out, lse_ref):
    length = q_ref.shape[0]
    cosine, slo, shi = cos_ref[...], slo_ref[...], shi_ref[...]
    q_low = (rotate_pair(q_ref[...], cosine, slo, shi).astype(BF16)) * jnp.asarray(HEAD_DIM**-0.5, BF16)
    k_low = rotate_pair(k_ref[...], cosine, slo, shi).astype(BF16)
    v_low = v_ref[...].astype(BF16)
    q_out[...] = q_low
    k_out[...] = k_low
    v_out[...] = v_low
    lane = lax.broadcasted_iota(jnp.int32, (1, PAIR), 1)
    v_t = v_low.T
    for b in range(length // blk):
        rows = slice(b * blk, (b + 1) * blk)
        keys = (b + 1) * blk
        mask = allowed_mask(segc_ref[:keys, :1], segr_ref[:1, rows], 0, keys, b * blk, blk)
        outs = []
        for h in range(2):
            mine = (lane < HEAD_DIM) if h == 0 else (lane >= HEAD_DIM)
            qh = jnp.where(mine, q_low[rows], jnp.zeros((), BF16))
            s = jnp.where(mask, nt(k_low[:keys], qh), NEG)
            top = jnp.max(s, axis=0, keepdims=True)
            e = jnp.exp(s - top)
            total = jnp.sum(e, axis=0, keepdims=True)
            p = (e * (1.0 / total)).astype(BF16)
            lse_ref[0, h : h + 1, rows] = top + jnp.log(total)
            outs.append(nn(v_t[h * HEAD_DIM : (h + 1) * HEAD_DIM, :keys], p))
        o_ref[rows, :] = jnp.concatenate(outs, 0).T.astype(BF16)


def attend(mixed, tables, seg_col, seg_row, blk):
    length, wide = mixed.shape
    heads_wide = wide // 3
    pairs = heads_wide // PAIR
    col = lambda off: pl.BlockSpec((length, PAIR), lambda p: (0, off + p))
    fixed = lambda shape: pl.BlockSpec(shape, lambda p: (0, 0))
    return pl.pallas_call(
        functools.partial(attend_kernel, blk),
        grid=(pairs,),
        in_specs=[col(0), col(pairs), col(2 * pairs)]
        + [fixed((length, PAIR))] * 3
        + [fixed((length, 1)), fixed((1, length))],
        out_specs=[col(0)] * 4 + [pl.BlockSpec((1, 2, length), lambda p: (p, 0, 0))],
        out_shape=[jax.ShapeDtypeStruct((length, heads_wide), BF16)] * 4
        + [jax.ShapeDtypeStruct((pairs, 2, length), F32)],
        compiler_params=pltpu.CompilerParams(vmem_limit_bytes=56 << 20),
        name="attend",
    )(mixed, mixed, mixed, *tables, seg_col, seg_row)


def attend_back_kernel(blk, q_ref, k_ref, v_ref, g_ref, lse_ref, cos_ref, slo_ref, shi_ref,
                       segc_ref, segr_ref, dq_ref, dk_ref, dv_ref, dk_acc, dv_acc):
    length = q_ref.shape[0]
    q_low, k_low, v_low, g_low = q_ref[...], k_ref[...], v_ref[...], g_ref[...]
    lane = lax.broadcasted_iota(jnp.int32, (1, PAIR), 1)
    k_t = k_low.T
    zero = jnp.zeros((), BF16)
    cosine, slo, shi = cos_ref[...], slo_ref[...], shi_ref[...]
    first = lane < HEAD_DIM
    count = length // blk
    for b in reversed(range(count)):
        rows = slice(b * blk, (b + 1) * blk)
        keys = (b + 1) * blk
        mask = allowed_mask(segc_ref[:keys, :1], segr_ref[:1, rows], 0, keys, b * blk, blk)
        dq_t, dk_h, dv_h = [], [], []
        for h in range(2):
            mine = first if h == 0 else jnp.logical_not(first)
            qh = jnp.where(mine, q_low[rows], zero)
            gh = jnp.where(mine, g_low[rows], zero)
            s = jnp.where(mask, nt(k_low[:keys], qh), NEG)
            p = jnp.exp(s - lse_ref[0, h : h + 1, rows])
            dp = nt(v_low[:keys], gh)
            delta = jnp.sum(p * dp, axis=0, keepdims=True)
            ds = (p * (dp - delta)).astype(BF16)
            dq_t.append(nn(k_t[h * HEAD_DIM : (h + 1) * HEAD_DIM, :keys], ds))
            dk_h.append(nn(ds, q_low[rows]))
            dv_h.append(nn(p.astype(BF16), g_low[rows]))
        dk_new = jnp.where(first, dk_h[0], dk_h[1])
        dv_new = jnp.where(first, dv_h[0], dv_h[1])
        if b == count - 1:
            dk_acc[...] = dk_new
            dv_acc[...] = dv_new
        else:
            dk_acc[:keys] += dk_new
            dv_acc[:keys] += dv_new
        dq = jnp.concatenate(dq_t, 0).T * (HEAD_DIM**-0.5)
        dq_ref[rows, :] = rotate_pair(dq, cosine[rows], -slo[rows], -shi[rows]).astype(BF16)
    dk_ref[...] = rotate_pair(dk_acc[...], cosine, -slo, -shi).astype(BF16)
    dv_ref[...] = dv_acc[...].astype(BF16)


def attend_back(q, k, v, g, lse, tables, seg_col, seg_row, blk):
    length, heads_wide = q.shape
    pairs = heads_wide // PAIR
    col = pl.BlockSpec((length, PAIR), lambda p: (0, p))
    fixed = lambda shape: pl.BlockSpec(shape, lambda p: (0, 0))
    return pl.pallas_call(
        functools.partial(attend_back_kernel, blk),
        grid=(pairs,),
        in_specs=[col] * 4
        + [pl.BlockSpec((1, 2, length), lambda p: (p, 0, 0))]
        + [fixed((length, PAIR))] * 3
        + [fixed((length, 1)), fixed((1, length))],
        out_specs=[col] * 3,
        out_shape=[jax.ShapeDtypeStruct((length, heads_wide), BF16)] * 3,
        scratch_shapes=[pltpu.VMEM((length, PAIR), F32)] * 2,
        compiler_params=pltpu.CompilerParams(vmem_limit_bytes=56 << 20),
        name="attend_back",
    )(q, k, v, g, lse, *tables, seg_col, seg_row)


def pick(x, index, axis=0):
    return lax.dynamic_index_in_dim(x, index, axis, keepdims=False)


def shift(x, offset, count):
    return lax.ppermute(x, "shard", [(i, (i + offset) % count) for i in range(count)])


def gather_row(x, count, me):
    half = x.shape[0] // 2
    out = jnp.zeros((count,) + x.shape, x.dtype)
    out = lax.dynamic_update_slice(out, x[None], (me, 0, 0))
    fore = aft = x
    for step in range(1, count // 2):
        fore = shift(fore, 1, count)
        aft = shift(aft, -1, count)
        out = lax.dynamic_update_slice(out, fore[None], ((me - step) % count, 0, 0))
        out = lax.dynamic_update_slice(out, aft[None], ((me + step) % count, 0, 0))
    far = (me + count // 2) % count
    fore = shift(fore[:half], 1, count)
    aft = shift(aft[half:], -1, count)
    out = lax.dynamic_update_slice(out, fore[None], (far, 0, 0))
    out = lax.dynamic_update_slice(out, aft[None], (far, half, 0))
    return out.reshape(count * x.shape[0], x.shape[1])


def scatter_row(x, count, me):
    x = x.reshape(count, x.shape[0] // count, x.shape[1])
    half = x.shape[1] // 2

    def block(step):
        return pick(x, (me + step) % count)

    far = block(count // 2)
    fore = shift(far[:half], 1, count)
    aft = shift(far[half:], -1, count)
    for step in range(count // 2 - 1, 0, -1):
        ahead, behind = block(step).astype(F32), block(-step).astype(F32)
        if fore.shape[0] == half:
            ahead = jnp.concatenate([ahead[:half] + fore.astype(F32), ahead[half:]], 0)
            behind = jnp.concatenate([behind[:half], behind[half:] + aft.astype(F32)], 0)
        else:
            ahead = ahead + fore.astype(F32)
            behind = behind + aft.astype(F32)
        fore = shift(ahead.astype(BF16), 1, count)
        aft = shift(behind.astype(BF16), -1, count)
    return block(0).astype(F32) + fore.astype(F32) + aft.astype(F32)


def scatter_direct(x, count, me):
    x = x.reshape(count, x.shape[0] // count, x.shape[1])
    out = pick(x, me).astype(F32)
    for step in range(1, count):
        out = out + shift(pick(x, (me + step) % count), step, count).astype(F32)
    return out


def gather_small(x, count, me):
    out = lax.dynamic_update_slice(jnp.zeros((count,) + x.shape, x.dtype), x[None], (me, 0))
    for step in range(1, count):
        out = lax.dynamic_update_slice(out, shift(x, step, count)[None], ((me - step) % count, 0))
    return out


def swap_blocks(x, axis, count, me):
    out = jnp.zeros(x.shape, x.dtype)

    def put(out, block, place):
        start = [0] * x.ndim
        start[axis] = place
        return lax.dynamic_update_slice(out, jnp.expand_dims(block, axis), start)

    out = put(out, pick(x, me, axis), me)
    for step in range(1, count):
        block = shift(pick(x, (me + step) % count, axis), step, count)
        out = put(out, block, (me - step) % count)
    return out


def flip(x, mask, reps):
    return lax.ppermute(x, "rep", [(i, i ^ mask) for i in range(reps)])


def reduce_chips(x, rep, reps):
    lead, rows, cols = x.shape
    chips = reps // 2
    x = x.reshape(lead, chips, rows // chips, cols)
    mine = rep >> 1
    arrived = [flip(pick(x, mine ^ mask, 1), 2 * mask, reps) for mask in range(1, chips)]

    def total():
        out = pick(x, mine, 1).astype(F32)
        for term in arrived:
            out = out + term.astype(F32)
        return out.astype(BF16)

    return total


def step_bits(reps):
    bits = list(range((reps // 2).bit_length() - 1))
    return bits, bits[::-1]


def spread(x, reps):
    half = x.shape[1] // 2
    own = []
    parts = [x[None, :, :half], x[None, :, half:]]
    steps = step_bits(reps)
    for step in range(len(steps[0])):
        last = step == len(steps[0]) - 1
        got = [flip(parts[i], 2 << steps[i][step], reps) for i in range(2)]
        if last:
            own = [parts[0], got[0], parts[1], got[1]]
        else:
            parts = [jnp.concatenate(pair, 0) for pair in zip(parts, got)]
    return own + [flip(piece, 1, reps) for piece in own]


def assemble(pieces, rep, wide):
    some, lead, tile, cols = pieces[0].shape
    chips = 2 * some
    groups, width = (1, 2 * cols * lead) if wide else (lead, 2 * cols)
    table = []
    for order in step_bits(2 * chips):
        masks = [0]
        for bit in order:
            masks += [m ^ (1 << bit) for m in masks]
        table += masks

    def kernel(table_ref, *refs):
        out = refs[-1]
        core = table_ref[2 * chips]
        for i in range(4):

            @pl.when(pl.program_id(0) == i)
            def _(i=i):
                for side, ref in ((core, refs[i]), (1 - core, refs[4 + i])):
                    for l in range(lead):
                        at = pl.multiple_of(side * cols + (l * 2 * cols if wide else 0), 128)
                        out[0 if wide else l, 0, :, pl.ds(at, cols)] = ref[0, l].astype(F32)

    def source(i):
        return pl.BlockSpec(
            (1, lead, tile, cols),
            lambda p, j, t: (jnp.where(p == i, j, jnp.where(p < i, 0, some - 1)), 0, 0, 0),
        )

    out = pl.pallas_call(
        kernel,
        grid_spec=pltpu.PrefetchScalarGridSpec(
            num_scalar_prefetch=1,
            grid=(4, some),
            in_specs=[source(i) for i in range(4)] * 2,
            out_specs=pl.BlockSpec(
                (groups, 1, tile, width), lambda p, j, t: (0, t[p * some + j], p // 2, 0)
            ),
        ),
        out_shape=jax.ShapeDtypeStruct((groups, chips, 2 * tile, width), F32),
        compiler_params=pltpu.CompilerParams(vmem_limit_bytes=48 << 20),
        name="assemble",
    )(jnp.concatenate([jnp.asarray(table, jnp.int32) ^ (rep >> 1), (rep & 1)[None]]), *pieces)
    return out.reshape(groups * chips * 2 * tile, width)


def lay_out(x, wide):
    reps, lead, rows, cols = x.shape
    tile = max(8, rows // 2)
    groups, width = (1, 2 * cols * lead) if wide else (lead, 2 * cols)

    def kernel(x_ref, out):
        for side in range(2):
            for l in range(lead):
                at = side * cols + (l * 2 * cols if wide else 0)
                out[0 if wide else l, 0, :, at : at + cols] = x_ref[side, l].astype(F32)

    out = pl.pallas_call(
        kernel,
        grid=(reps // 2, rows // tile),
        in_specs=[pl.BlockSpec((2, lead, tile, cols), lambda p, t: (p, 0, t, 0))],
        out_specs=pl.BlockSpec((groups, 1, tile, width), lambda p, t: (0, p, t, 0)),
        out_shape=jax.ShapeDtypeStruct((groups, reps // 2, rows, width), F32),
        compiler_params=pltpu.CompilerParams(vmem_limit_bytes=48 << 20),
        name="place",
    )(x)
    return out.reshape(groups * (reps // 2) * rows, width)


def hold(*xs):
    return lax.optimization_barrier(xs)


def local(
    tokens,
    segments,
    positions,
    norm_gain,
    norm_shift,
    inproj_weight,
    inproj_bias,
    outproj_weight,
    outproj_bias,
    expand_weight,
    expand_bias,
    shrink_weight,
    shrink_bias,
    out_grad,
):
    span, width = tokens.shape[1:]
    count = lax.axis_size("shard")
    reps = lax.axis_size("rep")
    bits = reps.bit_length() - 1
    me = lax.axis_index("shard")
    rep = lax.axis_index("rep")
    core = rep & 1
    length = span * count
    part = width // count
    inner = expand_weight.shape[0]
    sub = part // reps

    kind_of = np.zeros((count, 3), np.int32)
    forward = [[(s, (3 * s + j) % count) for s in range(count)] for j in range(3)]
    for s in range(count):
        for j in range(3):
            kind_of[(3 * s + j) % count, j] = (3 * s + j) // count
    round_of = np.argsort(kind_of, 1).astype(np.int32)

    packed = jnp.concatenate([norm_gain, norm_shift, outproj_bias, shrink_bias, inproj_bias])
    packed = gather_small(packed, count, me)
    gain, shift_all, outbias, shrbias = (
        packed[:, i * part : (i + 1) * part].reshape(width).astype(F32) for i in range(4)
    )
    inbias = packed[:, 4 * part :].reshape(3, count, part)
    inbias = pick(inbias, me, 1).reshape(3 * part).astype(F32)

    slices = lax.dynamic_slice_in_dim(inproj_weight.reshape(3, part, width), rep * sub, sub, 1)
    arrived = jnp.stack([lax.ppermute(slices[j], "shard", forward[j]) for j in range(3)])
    my_rounds = pick(jnp.asarray(round_of), me)
    arrived = jnp.stack([pick(arrived, my_rounds[k]) for k in range(3)])
    in_w = lax.all_gather(arrived, "rep", axis=1, tiled=True).reshape(3 * part, width)
    down = jnp.concatenate(
        [
            lax.dynamic_slice_in_dim(shrink_weight, rep * sub, sub, 0).reshape(sub, count, inner),
            lax.dynamic_slice_in_dim(outproj_weight, rep * sub, sub, 0).reshape(sub, count, part),
        ],
        2,
    )
    down = swap_blocks(jnp.transpose(down, (1, 0, 2)), 0, count, me)
    shrink_w = lax.all_gather(down[:, :, :inner], "rep", axis=1, tiled=True).reshape(width, inner)
    out_w = lax.all_gather(down[:, :, inner:], "rep", axis=1, tiled=True).reshape(width, part)

    residual = tokens.reshape(span, width).astype(F32)
    row_mean = jnp.mean(residual, -1, keepdims=True)
    centered = residual - row_mean
    row_var = jnp.mean(centered * centered, -1, keepdims=True)
    inv_std = lax.rsqrt(row_var + 1e-05)
    xhat = centered * inv_std
    normed_own = (xhat * gain + shift_all).astype(BF16)
    normed = gather_row(normed_own, count, me)

    grad_own = out_grad.reshape(span, width)
    grads = gather_row(grad_own, count, me)

    seg = segments.reshape(length)
    starts = jnp.sum((seg[None, :] < seg[:, None]).astype(jnp.int32), 1)
    place = (jnp.arange(length, dtype=jnp.int32) - starts).astype(F32)
    lane = jnp.arange(PAIR) % HEAD_DIM
    inverse_freq = 10000.0 ** (-(lane % (ROT // 2)).astype(F32) * 2.0 / ROT)
    angle = place[:, None] * inverse_freq[None, :]
    sine = jnp.sin(angle)
    tables = (
        jnp.where(lane < ROT, jnp.cos(angle), 1.0),
        jnp.where(lane < ROT // 2, -sine, 0.0),
        jnp.where((lane >= ROT // 2) & (lane < ROT), sine, 0.0),
    )
    seg_col, seg_row = seg[:, None], seg[None, :]
    blk = min(256, length)
    back = [[(b, a) for a, b in pairs] for pairs in forward]

    def col_half(x, which):
        wide = x.shape[1] // 2
        return lax.dynamic_slice_in_dim(x, which * wide, wide, 1)

    def low_term(outputs, inputs, extra=None):
        out = tn(outputs, inputs)
        return (out if extra is None else out + extra.astype(F32)).astype(BF16)

    normed_mine, normed_other = col_half(normed, core), col_half(normed, 1 - core)
    expanded = nt(normed, expand_weight) + expand_bias.astype(F32)
    hidden, slope = gelu_parts(expanded)
    hidden, slope = hidden.astype(BF16), slope.astype(BF16)
    hidden_mine, hidden_other = col_half(hidden, core), col_half(hidden, 1 - core)
    normed_1, hidden = hold(normed, hidden)
    mixed = nt(normed_1, in_w) + inbias
    attended, q_low, k_low, v_low, lse = attend(mixed, tables, seg_col, seg_row, blk)
    hidden_1, attended = hold(hidden, attended)
    branches = (nt(hidden_1, shrink_w) + nt(attended, out_w)).astype(BF16)
    branches_sum = scatter_direct(branches, count, me)

    grads, branches = hold(grads, branches)
    blocks = inner // part
    g_out = tn(grads, attended).astype(BF16)
    g_out_1 = lax.psum_scatter(
        g_out.reshape(count, part, part), "rep", scatter_dimension=1, tiled=True
    )
    grads, g_out = hold(grads, g_out)
    shr_send = low_term(grads, hidden_other)
    shr_arrived = flip(shr_send, 1, reps)
    grads_1, shr_send = hold(grads, shr_send)
    d_up = (nn(grads_1, shrink_w) * slope.astype(F32)).astype(BF16)
    grads_2, d_up = hold(grads_1, d_up)
    shr_sum = low_term(grads_2, hidden_mine, shr_arrived)
    shr_total = reduce_chips(shr_sum.reshape(count, part, inner // 2), rep, reps)
    d_up, shr_sum = hold(d_up, shr_sum)
    exp_send = low_term(d_up, normed_other)
    exp_arrived = flip(exp_send, 1, reps)
    grads_3, exp_send = hold(grads_2, exp_send)
    d_att = nn(grads_3, out_w).astype(BF16)
    d_up_1, d_att = hold(d_up, d_att)
    exp_sum = low_term(d_up_1, normed_mine, exp_arrived)
    exp_total = reduce_chips(exp_sum.reshape(blocks, part, width // 2), rep, reps)

    d_up_2, exp_sum, g_out_1 = hold(d_up_1, exp_sum, g_out_1)
    g_out = jnp.transpose(swap_blocks(g_out_1, 0, count, me), (1, 0, 2)).reshape(sub, width)
    d_normed = nn(d_up_2, expand_weight)
    g_shr = shr_total()
    d_att, d_normed, g_shr = hold(d_att, d_normed, g_shr)
    g_shr = swap_blocks(g_shr, 0, count, me)
    g_shr = lax.all_gather(g_shr, "rep", axis=0)
    d_q, d_k, d_v = attend_back(q_low, k_low, v_low, d_att, lse, tables, seg_col, seg_row, blk)
    d_mixed = jnp.concatenate([d_q, d_k, d_v], 1)
    in_send = low_term(d_mixed, normed_other)
    in_arrived = flip(in_send, 1, reps)
    d_mixed_1, in_send = hold(d_mixed, in_send)
    b_out = jnp.sum(lax.dynamic_slice_in_dim(grads_3, me * part, part, 1), 0, dtype=F32)
    b_exp = jnp.sum(d_up_2, 0, dtype=F32)
    b_in = jnp.sum(d_mixed_1, 0, dtype=F32)
    d_mixed_1, b_in = hold(d_mixed_1, b_in)
    in_sum = low_term(d_mixed_1, normed_mine, in_arrived)
    in_total = reduce_chips(in_sum.reshape(3, part, width // 2), rep, reps)
    d_mixed_2, in_sum = hold(d_mixed_1, in_sum)
    g_exp = exp_total()
    exp_pieces = spread(g_exp, reps)
    d_mixed_2, g_exp = hold(d_mixed_2, g_exp)
    d_normed = d_normed + nn(d_mixed_2, in_w)
    both = jnp.stack([jnp.sum(d_normed * normed.astype(F32), 0), jnp.sum(d_normed, 0)])
    d_normed = d_normed.astype(BF16)
    d_normed = scatter_row(d_normed, count, me)
    kinds = pick(jnp.asarray(kind_of), me)
    g_in = in_total()
    g_in = jnp.stack([lax.ppermute(pick(g_in, kinds[j]), "shard", back[j]) for j in range(3)])
    in_pieces = spread(g_in, reps)

    both = jnp.sum(swap_blocks(both.reshape(2, count, part), 1, count, me), 1)
    sums = jnp.concatenate([both[0], both[1], b_out, b_exp, b_in])

    g_out = lax.all_gather(g_out, "rep", axis=0, tiled=True).astype(F32)
    g_shr = lay_out(g_shr, True)
    g_exp = assemble(exp_pieces, rep, False)
    g_in = assemble(in_pieces, rep, False)
    block_output = (residual + (branches_sum + (outbias + shrbias))).astype(BF16)

    d_hat = d_normed * gain
    token_grad = grad_own.astype(F32) + inv_std * (
        d_hat
        - jnp.mean(d_hat, -1, keepdims=True)
        - xhat * jnp.mean(d_hat * xhat, -1, keepdims=True)
    )

    for bit in range(bits):
        sums = sums + flip(sums, 1 << bit, reps)
    b_norm, b_shift, b_out = sums[:part], sums[part : 2 * part], sums[2 * part : 3 * part]
    b_gain = (b_norm - norm_shift.astype(F32) * b_shift) / norm_gain.astype(F32)
    b_exp, b_in = sums[3 * part : 3 * part + inner], sums[3 * part + inner :].reshape(3, part)
    b_in = jnp.concatenate([lax.ppermute(pick(b_in, kinds[j]), "shard", back[j]) for j in range(3)])

    return (
        block_output[None],
        token_grad[None],
        b_gain,
        b_shift,
        g_in,
        b_in,
        g_out,
        b_out,
        g_exp,
        b_exp,
        g_shr,
        b_out,
    )


def solution(mesh):
    in_specs = (
        P("rep", "shard", None),
        P("rep", None),
        P("rep", "shard"),
        P("shard"),
        P("shard"),
        P("shard", None),
        P("shard"),
        P("shard", None),
        P("shard"),
        P("shard", None),
        P("shard"),
        P("shard", None),
        P("shard"),
        P("rep", "shard", None),
    )
    out_specs = (
        P("rep", "shard", None),
        P("rep", "shard", None),
        P("shard"),
        P("shard"),
        P("shard", None),
        P("shard"),
        P("shard", None),
        P("shard"),
        P("shard", None),
        P("shard"),
        P("shard", None),
        P("shard"),
    )

    return jax.shard_map(local, mesh=mesh, in_specs=in_specs, out_specs=out_specs, check_vma=False)
```
